256 devices in a mesh: row: 32 (over y, z), col: 8 (over x, core).
Axes of the slice: x: 4, y: 4, z: 8, core: 2. Of those that a mesh axis runs over, the one named last changes fastest.
Arguments:
- panel: bfloat16 [2, 32, 512, 8, 512], P(None, 'row', None, 'col'), may hold values from -0.1875 to 0.1875
- rhs: float32 [2, 32, 512, 2048], P(None, 'row', None, 'col'), may hold values from -6 to 6
- inverse: bfloat16 [8, 512, 512], replicated, as said below
Outputs:
- solved: float32 [8, 512, 2048], P(None, None, 'col')
- remainder: float32 [2, 32, 512, 2048], P(None, 'row', None, 'col')
The draws below stay inside these ranges and needn't reach their ends.
Inputs may be any that keep to these rules, and one draw needn't show every extreme that they name: Each block of inverse is lower triangular with a positive diagonal.
All inputs are finite; a program needn't handle non-finite values.
Results may differ from the reference program's by a relative error of at most 0.008.
Values may be sent and summed in bfloat16 or wider, within the bound.
No kernel may reach another device: no remote copies, remote signals or barrier semaphores. Data moves between devices by JAX's collectives and lax.ppermute only.
A program may use at most 128 MiB of HBM per device.

```python
import math
import jax
import jax.numpy as jnp

B = 512
NRHS = 2048
RB = 2
STEPS = 8
OFF = 24
NB = 64
N_ROW = 32


def draw_inverse(key, part):
    first, second = jax.random.split(jax.random.fold_in(key, 7), 2)
    diagonal = jax.random.uniform(first, (STEPS, B), minval=0.6, maxval=1.4)
    spread = jax.random.normal(second, (STEPS, B, B)) * (0.7 / math.sqrt(B))
    lower = jnp.tril(spread, -1) + diagonal[:, :, None] * jnp.eye(B, dtype=jnp.float32)[None]
    return lower.astype(jnp.bfloat16)


def shard_levels(rng, shape, cuts, smallest, top_value):
    gain, own = 1.0, jax.random.fold_in(rng, 6)
    for dim, blocks in cuts:
        heights = jnp.exp(jax.random.uniform(jax.random.fold_in(own, dim), (blocks,), jnp.float32, smallest / len(cuts), top_value / len(cuts)))
        gain = gain * jnp.repeat(heights, shape[dim] // blocks).reshape([-1 if axis == dim else 1 for axis in range(len(shape))])
    return gain


def gaussian(stream_key, shape, scale, limit, pieces=(), kind=jnp.bfloat16):
    factor_of = shard_levels(stream_key, shape, pieces, -0.22, 0.18) if pieces else 1.0
    entries = jax.random.normal(stream_key, shape, jnp.float32) * scale * factor_of
    return jnp.minimum(jnp.maximum(entries, -limit), limit).astype(kind)


def setup_inputs(seed: int = 0) -> dict:
    splits = jax.random.split(jax.random.key(seed), 4)
    return {
        "panel": gaussian(splits[0], (RB, N_ROW, B, STEPS, B), (B * STEPS // 4) ** -0.5, 0.1875, ((1, 32), (3, 8))),
        "rhs": gaussian(splits[1], (RB, N_ROW, B, NRHS), 1.0, 6.0, ((1, 32), (3, 8)), jnp.float32),
        "inverse": draw_inverse(jax.random.fold_in(splits[3], 71), 0),
    }


def reference(panel, rhs, inverse):
    blocks = panel.reshape(NB, B, STEPS, B)
    right = rhs.reshape(NB, B, NRHS)
    solved_list = []
    low_list = []
    for k in range(STEPS):
        base = right[OFF + k]
        if k > 0:
            left = blocks[OFF + k, :, :k, :].reshape(B, k * B)
            lower = jnp.stack(low_list, axis=0).reshape(k * B, NRHS)
            base = base - jnp.dot(left, lower, preferred_element_type=jnp.float32)
        fresh = jnp.dot(inverse[k], base.astype(jnp.bfloat16), preferred_element_type=jnp.float32)
        solved_list.append(fresh)
        low_list.append(fresh.astype(jnp.bfloat16))
    solved = jnp.stack(solved_list, axis=0)
    lower_all = jnp.stack(low_list, axis=0).reshape(STEPS * B, NRHS)
    block_rows = jnp.arange(NB, dtype=jnp.int32)
    block_cols = jnp.arange(STEPS, dtype=jnp.int32)
    keep = (block_cols[None, :] + OFF < block_rows[:, None]).astype(jnp.bfloat16)
    masked = blocks * keep[:, None, :, None]
    update = jnp.dot(masked.reshape(NB * B, STEPS * B), lower_all, preferred_element_type=jnp.float32)
    remainder = right - update.reshape(NB, B, NRHS)
    return solved, remainder.reshape(RB, N_ROW, B, NRHS)
```

```python
import jax
import jax.numpy as jnp
from jax import lax
from jax.experimental import pallas as pl
from jax.experimental.pallas import tpu as pltpu
from jax.sharding import PartitionSpec as P


NY, NZ, NX = 4, 8, 4
NT = (((1,), (1,)), ((), ()))
BF = jnp.bfloat16
F32 = jnp.float32


def row_of(y, z):
    return (y % NY) * NZ + z % NZ


def shift_y(d):
    return [(row_of(y, z), row_of(y + d, z)) for y in range(NY) for z in range(NZ)]


def shift_z(d):
    return [(row_of(y, z), row_of(y, z + d)) for y in range(NY) for z in range(NZ)]


def hop_z(t):
    return [(row_of(y, t - 1), row_of(y, t)) for y in range(NY)]


def hop_z_early(t):
    return hop_z(t) + [(row_of(0, t + 3), row_of(0, t + 4))]


def shift_x(d):
    n = 2 * NX
    return [(i, (i + 2 * d) % n) for i in range(n)]


SWAP = [(i, i ^ 1) for i in range(2 * NX)]


def after(x, *deps):
    return lax.optimization_barrier((x, *deps))[0]


def gather_x(block):
    half = block.shape[0] // 2
    left = lax.ppermute(block, "col", shift_x(1))
    right = lax.ppermute(block, "col", shift_x(-1))
    far_a = lax.ppermute(left[:half], "col", shift_x(1))
    far_b = lax.ppermute(right[half:], "col", shift_x(-1))
    mine = jnp.stack([block, left, right, jnp.concatenate([far_a, far_b])])
    other = lax.ppermute(mine, "col", SWAP)
    return mine, other


def pick(own, mine, other):
    return jnp.where(own, mine, other)


def early_kernel(sc, base, solved, mine, other, out):
    j = pl.program_id(0)

    @pl.when(j == 0)
    def _():
        out[...] = base[...].astype(F32)

    block = pick(sc[8 + j] == 1, mine[0], other[0])
    out[...] -= lax.dot_general(solved[0], block, NT, preferred_element_type=F32)


def early(sc, base, solved, mine, other):
    n = solved.shape[0]
    c, b = base.shape
    return pl.pallas_call(
        early_kernel,
        out_shape=jax.ShapeDtypeStruct((c, b), F32),
        grid_spec=pltpu.PrefetchScalarGridSpec(
            num_scalar_prefetch=1,
            grid=(n,),
            in_specs=[
                pl.BlockSpec((c, b), lambda j, sc: (0, 0)),
                pl.BlockSpec((1, c, b), lambda j, sc: (j, 0, 0)),
                pl.BlockSpec((1, b, b), lambda j, sc: (sc[j], 0, 0)),
                pl.BlockSpec((1, b, b), lambda j, sc: (sc[j], 0, 0)),
            ],
            out_specs=pl.BlockSpec((c, b), lambda j, sc: (0, 0)),
        ),
        cost_estimate=pl.CostEstimate(
            flops=2 * n * c * b * b, bytes_accessed=4 * n * b * b, transcendentals=0
        ),
        name="early",
    )(sc, base, solved, mine, other)


def step_kernel(t, sc, acc, last, mine, other, inv, out):
    block = pick(sc[8 + t - 1] == 1, mine[0], other[0])
    base = acc[...] - lax.dot_general(last[...], block, NT, preferred_element_type=F32)
    fresh = lax.dot_general(base.astype(BF), inv[0], NT, preferred_element_type=F32)
    out[...] = fresh.astype(BF)


def step(t, sc, acc, last, mine, other, inverse):
    c, b = acc.shape
    return pl.pallas_call(
        lambda *refs: step_kernel(t, *refs),
        out_shape=jax.ShapeDtypeStruct((c, b), BF),
        grid_spec=pltpu.PrefetchScalarGridSpec(
            num_scalar_prefetch=1,
            grid=(1,),
            in_specs=[
                pl.BlockSpec((c, b), lambda i, sc: (0, 0)),
                pl.BlockSpec((c, b), lambda i, sc: (0, 0)),
                pl.BlockSpec((1, b, b), lambda i, sc: (sc[t - 1], 0, 0)),
                pl.BlockSpec((1, b, b), lambda i, sc: (sc[t - 1], 0, 0)),
                pl.BlockSpec((1, b, b), lambda i, sc: (t, 0, 0)),
            ],
            out_specs=pl.BlockSpec((c, b), lambda i, sc: (0, 0)),
        ),
        cost_estimate=pl.CostEstimate(
            flops=4 * c * b * b, bytes_accessed=6 * b * b, transcendentals=0
        ),
        name="step",
    )(sc, acc, last, mine, other, inverse)


def first_kernel(base, inv, out):
    out[...] = lax.dot_general(
        base[...], inv[0], NT, preferred_element_type=F32
    ).astype(BF)


def first(base, inverse):
    c, b = base.shape
    return pl.pallas_call(
        first_kernel,
        out_shape=jax.ShapeDtypeStruct((c, b), BF),
        grid=(1,),
        in_specs=[
            pl.BlockSpec((c, b), lambda i: (0, 0)),
            pl.BlockSpec((1, b, b), lambda i: (0, 0, 0)),
        ],
        out_specs=pl.BlockSpec((c, b), lambda i: (0, 0)),
        name="first",
    )(base, inverse)


def final_kernel(sc, solved, ident, mine0, other0, mine1, other1, rhs, out_s, out_r):
    k = pl.program_id(0)
    low = solved[...].reshape(-1, solved.shape[-1])
    own = sc[8 + k] == 1

    @pl.when(k == 0)
    def _():
        out_r[...] = rhs[...]

    out_s[0] = lax.dot_general(ident[...], low, NT, preferred_element_type=F32)
    block1 = pick(own, mine1[0], other1[0])
    out_r[1, 0] -= lax.dot_general(block1, low, NT, preferred_element_type=F32)

    @pl.when(k < sc[16])
    def _():
        block0 = pick(own, mine0[0], other0[0])
        out_r[0, 0] -= lax.dot_general(block0, low, NT, preferred_element_type=F32)


def final(sc, solved, gathered0, gathered1, rhs):
    q, steps, c, b = solved.shape
    ident = jnp.eye(b, dtype=BF)
    block = pl.BlockSpec((1, b, b), lambda k, sc: (sc[k], 0, 0))
    whole = pl.BlockSpec(rhs.shape, lambda k, sc: (0, 0, 0, 0))
    return pl.pallas_call(
        final_kernel,
        out_shape=(
            jax.ShapeDtypeStruct((steps, b, q * c), F32),
            jax.ShapeDtypeStruct(rhs.shape, F32),
        ),
        grid_spec=pltpu.PrefetchScalarGridSpec(
            num_scalar_prefetch=1,
            grid=(steps,),
            in_specs=[
                pl.BlockSpec((q, 1, c, b), lambda k, sc: (0, k, 0, 0)),
                pl.BlockSpec((b, b), lambda k, sc: (0, 0)),
                block,
                block,
                block,
                block,
                whole,
            ],
            out_specs=(
                pl.BlockSpec((1, b, q * c), lambda k, sc: (k, 0, 0)),
                whole,
            ),
        ),
        name="final",
    )(sc, solved, ident, *gathered0, *gathered1, rhs)


def on_device(panel, rhs, inverse):
    steps = inverse.shape[0]
    block = panel.shape[2]
    cols = rhs.shape[3]
    quarter = cols // NY
    row = lax.axis_index("row")
    col = lax.axis_index("col")
    y, z = row // NZ, row % NZ
    x, core = col // 2, col % 2

    j = jnp.arange(steps, dtype=jnp.int32)
    away = (j // 2 - x) % NX
    place = jnp.where(away == 0, 0, jnp.where(away == 3, 1, jnp.where(away == 1, 2, 3)))
    own = (j % 2 == core).astype(jnp.int32)
    limit = jnp.where(y == NY - 1, z, 0).astype(jnp.int32)
    sc = jnp.concatenate([place.astype(jnp.int32), own, limit[None]])

    panel0 = panel[0, 0, :, 0, :]
    zt = rhs[0, 0].astype(BF).T
    zq = [zt[i * quarter : (i + 1) * quarter] for i in range(NY)]
    up = lax.ppermute(jnp.concatenate([panel0, zq[0], zq[1]]), "row", shift_y(1))
    down = lax.ppermute(jnp.concatenate([panel0, zq[2]]), "row", shift_y(-1))
    half = block // 2
    up2 = lax.ppermute(
        jnp.concatenate([up[:half], up[block + quarter :]]), "row", shift_y(1)
    )
    down2 = lax.ppermute(down[half:block], "row", shift_y(-1))
    window = jnp.where(
        y == 3,
        panel0,
        jnp.where(
            y == 0,
            up[:block],
            jnp.where(y == 2, down[:block], jnp.concatenate([up2[:half], down2])),
        ),
    )
    base = jnp.where(
        y == 3,
        zq[3],
        jnp.where(
            y == 0,
            up[block : block + quarter],
            jnp.where(y == 2, down[block:], up2[half:]),
        ),
    )

    mine0, other0 = gather_x(window)

    fresh = first(base, inverse)
    own_s = fresh
    known = None
    acc = base.astype(F32)
    panel1 = after(panel[1, 0, :, 0, :], other0)
    mine1, other1 = gather_x(panel1)
    for t in range(1, steps):
        if t > 1:
            sent = lax.ppermute(known, "row", hop_z_early(t))
        last = lax.ppermute(fresh, "row", hop_z(t))
        if t > 1:
            acc = early(sc, base, sent, mine0, other0)
        fresh = step(t, sc, acc, last, mine0, other0, inverse)
        own_s = jnp.where(z == t, fresh, own_s)
        known = last[None] if t == 1 else jnp.concatenate([sent, last[None]])

    parts = [own_s]
    for d in range(NZ - 1, 0, -1):
        parts.append(lax.ppermute(own_s, "row", shift_z(d)))
    around = jnp.stack(parts)
    around = jnp.concatenate([around, around])
    every = lax.dynamic_slice_in_dim(around, (NZ - z) % NZ, NZ, 0)
    before = lax.ppermute(every, "row", shift_y(1))
    behind = lax.ppermute(every, "row", shift_y(-1))
    far_a = lax.ppermute(before[: NZ // 2], "row", shift_y(1))
    far_b = lax.ppermute(behind[NZ // 2 :], "row", shift_y(-1))
    far = jnp.concatenate([far_a, far_b])
    planes = jnp.stack([every, behind, far, before])
    planes = jnp.concatenate([planes, planes])
    solved = lax.dynamic_slice_in_dim(planes, (NY - y) % NY, NY, 0)

    return tuple(final(sc, solved, (mine0, other0), (mine1, other1), rhs))


def solution(mesh):
    placed = (P(None, "row", None, "col", None), P(None, "row", None, "col"), P())
    return jax.shard_map(
        on_device,
        mesh=mesh,
        in_specs=placed,
        out_specs=(P(None, None, "col"), P(None, "row", None, "col")),
        check_vma=False,
    )
```

```python
import jax
import jax.numpy as jnp
from jax import lax
from jax.experimental import pallas as pl
from jax.experimental.pallas import tpu as pltpu
from jax.sharding import PartitionSpec as P


NY, NZ, NX = 4, 8, 4
NT = (((1,), (1,)), ((), ()))
BF = jnp.bfloat16
F32 = jnp.float32


def row_of(y, z):
    return (y % NY) * NZ + z % NZ


def shift_y(d):
    return [(row_of(y, z), row_of(y + d, z)) for y in range(NY) for z in range(NZ)]


def from_plane(y, to):
    return [(row_of(y, z), row_of(to, z)) for z in range(NZ)]


def back_z(d, rows):
    return [(row_of(y, k), row_of(y, k - d)) for y in range(NY) for k in rows if k >= d]


def hop_z(t):
    return [(row_of(y, t - 1), row_of(y, t)) for y in range(NY)]


def hop_z_early(t):
    return hop_z(t) + [(row_of(0, t + 3), row_of(0, t + 4))]


def shift_x(d):
    n = 2 * NX
    return [(i, (i + 2 * d) % n) for i in range(n)]


SWAP = [(i, i ^ 1) for i in range(2 * NX)]


def after(x, *deps):
    return lax.optimization_barrier((x, *deps))[0]


VMEM = pl.BlockSpec(memory_space=pltpu.VMEM)
SMEM = pl.BlockSpec(memory_space=pltpu.SMEM)
LIMIT = 8 * 1024 * 1024
PLACE, KIND, ROWS, AT_Z, PLANE = 0, 8, 16, 17, 18


def in_vmem(x):
    return pltpu.with_memory_space_constraint(x, pltpu.VMEM)


def params(limit=LIMIT):
    return pltpu.CompilerParams(vmem_limit_bytes=limit)


def times_block(sc, j, low, blocks, use, flip=False):
    place = sc[PLACE + j]
    for kind, ref in enumerate(blocks):

        @pl.when(sc[KIND + j] == kind)
        def _():
            block = ref[place] if len(ref.shape) == 3 else ref[...]
            pair = (block, low) if flip else (low, block)
            use(lax.dot_general(*pair, NT, preferred_element_type=F32))


def early_kernel(sc, base, solved, *refs):
    *blocks, out = refs
    out[...] = base[...].astype(F32)

    def subtract(value):
        out[...] -= value

    @pl.loop(0, solved.shape[0])
    def _(j):
        times_block(sc, j, solved[j], blocks, subtract)


def early(sc, base, solved, blocks):
    n = solved.shape[0]
    c, b = base.shape
    return pl.pallas_call(
        early_kernel,
        out_shape=jax.ShapeDtypeStruct((c, b), F32),
        in_specs=[SMEM] + [VMEM] * (2 + len(blocks)),
        out_specs=VMEM,
        compiler_params=params(),
        cost_estimate=pl.CostEstimate(
            flops=2 * n * c * b * b, bytes_accessed=n * b * b, transcendentals=0
        ),
        name="early",
    )(sc, base, solved, *blocks)


def step_kernel(t, sc, acc, last, inv, *refs):
    *blocks, out, base = refs

    def subtract(value):
        base[...] = (acc[...] - value).astype(BF)

    times_block(sc, t - 1, last[...], blocks, subtract)
    out[...] = lax.dot_general(
        base[...], inv[...], NT, preferred_element_type=F32
    ).astype(BF)


def step(t, sc, acc, last, inv, blocks):
    c, b = acc.shape
    return pl.pallas_call(
        lambda *refs: step_kernel(t, *refs),
        out_shape=jax.ShapeDtypeStruct((c, b), BF),
        in_specs=[SMEM] + [VMEM] * (3 + len(blocks)),
        out_specs=VMEM,
        scratch_shapes=[pltpu.VMEM((c, b), BF)],
        compiler_params=params(),
        cost_estimate=pl.CostEstimate(
            flops=4 * c * b * b, bytes_accessed=2 * b * b, transcendentals=0
        ),
        name="step",
    )(sc, acc, last, inv, *blocks)


def first_kernel(base, inv, out):
    out[...] = lax.dot_general(
        base[...], inv[...], NT, preferred_element_type=F32
    ).astype(BF)


def first(base, inv):
    return pl.pallas_call(
        first_kernel,
        out_shape=jax.ShapeDtypeStruct(base.shape, BF),
        in_specs=[VMEM, VMEM],
        out_specs=VMEM,
        compiler_params=params(),
        name="first",
    )(base, inv)


def collect(sc, rows, own, before, after_own):
    c, b = own.shape
    names, arrays = {}, []

    def ref_of(x):
        if id(x) not in names:
            names[id(x)] = len(arrays)
            arrays.append(x)
        return names[id(x)]

    def source(z, k):
        if k == z:
            return ref_of(own), None
        if k > z:
            return ref_of(after_own[k - z - 1]), None
        at = 0
        for x in before[z]:
            if len(x.shape) == 2:
                if at == k:
                    return ref_of(x), None
                at += 1
            else:
                if at <= k < at + x.shape[0]:
                    return ref_of(x), k - at
                at += x.shape[0]

    plan = [[source(z, k) for k in rows] for z in range(NZ)]

    def kernel(sc, *refs):
        *ins, out = refs
        for z in range(NZ):

            @pl.when(sc[AT_Z] == z)
            def _():
                for i, (which, at) in enumerate(plan[z]):
                    out[i] = ins[which][...] if at is None else ins[which][at]

    return pl.pallas_call(
        kernel,
        out_shape=jax.ShapeDtypeStruct((len(rows), c, b), BF),
        in_specs=[SMEM] + [VMEM] * len(arrays),
        out_specs=VMEM,
        compiler_params=params(),
        cost_estimate=pl.CostEstimate(
            flops=0, bytes_accessed=4 * len(rows) * c * b, transcendentals=0
        ),
        name="collect",
    )(sc, *arrays)


def spread_y(rows):
    half = rows.shape[0] // 2
    before = lax.ppermute(rows, "row", shift_y(1))
    behind = lax.ppermute(rows, "row", shift_y(-1))
    far_a = lax.ppermute(before[:half], "row", shift_y(1))
    far_b = lax.ppermute(behind[half:], "row", shift_y(-1))
    return rows, behind, far_a, far_b, before


def final_kernel(start, sc, every, behind, far_a, far_b, before, *refs):
    blocks0, blocks1, rest = refs[:4], refs[4:8], refs[8:]
    rhs, (out_s, out_r, low, eye) = rest[0], rest[-4:]
    i = pl.program_id(0)
    c = every.shape[1]
    half = far_a.shape[0]

    @pl.when(i == 0)
    def _():
        out_r[...] = rhs[...]
        across = lax.broadcasted_iota(jnp.int32, eye.shape, 0)
        down = lax.broadcasted_iota(jnp.int32, eye.shape, 1)
        eye[...] = (across == down).astype(F32).astype(BF)

    def put(m, value):
        low[pl.ds(pl.multiple_of(sc[PLANE + m] * c, c), c), :] = value

    put(0, every[i])
    put(1, behind[i])
    put(3, before[i])

    @pl.when(i < half)
    def _():
        put(2, far_a[i])

    @pl.when(i >= half)
    def _():
        put(2, far_b[i - half])

    solved = low[...]
    out_s[0] = lax.dot_general(eye[...], solved, NT, preferred_element_type=F32)

    def remove(q):
        def use(value):
            out_r[q, 0] -= value

        return use

    k = start + i
    times_block(sc, k, solved, blocks1, remove(1), flip=True)

    @pl.when(k < sc[ROWS])
    def _():
        times_block(sc, k, solved, blocks0, remove(0), flip=True)


def final(start, sc, steps, pieces, blocks0, blocks1, rhs, out_s=None):
    n, c, b = pieces[0].shape
    cols = rhs.shape[3]
    args = [sc, *pieces, *blocks0, *blocks1, rhs]
    specs = [SMEM] + [VMEM] * (len(args) - 1)
    alias = {}
    if out_s is not None:
        alias = {len(args): 0}
        args.append(out_s)
        specs.append(pl.BlockSpec(memory_space=pl.ANY))
    return pl.pallas_call(
        lambda *refs: final_kernel(start, *refs),
        out_shape=(
            jax.ShapeDtypeStruct((steps, b, cols), F32),
            jax.ShapeDtypeStruct(rhs.shape, F32),
        ),
        grid=(n,),
        in_specs=specs,
        out_specs=(
            pl.BlockSpec((1, b, cols), lambda i: (start + i, 0, 0)),
            pl.BlockSpec(rhs.shape, lambda i: (0, 0, 0, 0)),
        ),
        scratch_shapes=[pltpu.VMEM((cols, b), BF), pltpu.VMEM((b, b), BF)],
        input_output_aliases=alias,
        compiler_params=params(2 * LIMIT),
        cost_estimate=pl.CostEstimate(
            flops=6 * n * b * b * cols,
            bytes_accessed=4 * n * b * cols,
            transcendentals=0,
        ),
        name="final",
    )(*args)


def on_device(panel, rhs, inverse):
    steps = inverse.shape[0]
    block = panel.shape[2]
    quarter = rhs.shape[3] // NY
    half = block // 2
    row = lax.axis_index("row")
    col = lax.axis_index("col")
    y, z = row // NZ, row % NZ
    x, core = col // 2, col % 2

    j = jnp.arange(steps, dtype=jnp.int32)
    away = (j // 2 - x) % NX
    place = jnp.where(away == 3, 1, jnp.where(away == 1, 2, 0))
    kind = (away == 2) + 2 * (j % 2 != core)
    limit = jnp.where(y == NY - 1, z, 0)
    plane = (jnp.arange(NY, dtype=jnp.int32) + y) % NY
    sc = jnp.concatenate(
        [place, kind.astype(jnp.int32), limit[None], z[None], plane]
    ).astype(jnp.int32)

    panel0 = panel[0, 0, :, 0, :]
    top, low = panel0[:half], panel0[half:]
    up_a = lax.ppermute(top, "row", from_plane(3, 0))
    down_b = lax.ppermute(low, "row", from_plane(3, 2))
    up_b = lax.ppermute(low, "row", from_plane(3, 0) + [(row_of(1, 0), row_of(2, 0))])
    down_a = lax.ppermute(top, "row", from_plane(3, 2) + [(row_of(0, 0), row_of(1, 0))])
    far_a = lax.ppermute(up_a, "row", from_plane(0, 1))
    far_b = lax.ppermute(down_b, "row", from_plane(2, 1))

    def by_plane(at0, at1, at2, at3):
        return jnp.where(
            y == 3, at3, jnp.where(y == 0, at0, jnp.where(y == 2, at2, at1))
        )

    window = jnp.concatenate(
        [by_plane(up_a, far_a, down_a, top), by_plane(up_b, far_b, down_b, low)]
    )

    left = lax.ppermute(window, "col", shift_x(1))
    right = lax.ppermute(window, "col", shift_x(-1))
    zt = rhs[0, 0].astype(BF).T
    zq = [zt[i * quarter : (i + 1) * quarter] for i in range(NY)]
    ready = [after(zq[0], up_a), after(zq[1], far_a), after(zq[2], down_b)]
    zr = [lax.ppermute(ready[i], "row", from_plane(3, i)) for i in range(NY - 1)]
    left, right, *zr = lax.optimization_barrier((left, right, *zr))
    base = by_plane(*zr, zq[3])

    def rest_of_x(own, left, right):
        far_a = lax.ppermute(left[:half], "col", shift_x(1))
        far_b = lax.ppermute(right[half:], "col", shift_x(-1))
        near = jnp.stack([own, left, right])
        near_other = lax.ppermute(near, "col", SWAP)
        far_a, far_b, near_other = lax.optimization_barrier((far_a, far_b, near_other))
        return near, jnp.concatenate([far_a, far_b]), near_other

    near, far, near_other = rest_of_x(window, left, right)
    far_other = lax.ppermute(far, "col", SWAP)
    blocks0 = [in_vmem(v) for v in (near, far, near_other, far_other)]

    panel1 = after(panel[1, 0, :, 0, :], far_other)
    left1 = lax.ppermute(panel1, "col", shift_x(1))
    right1 = lax.ppermute(panel1, "col", shift_x(-1))

    fresh = first(base, inverse[0])
    own_s = fresh
    acc = base.astype(F32)
    known = None
    before = {0: []}
    for t in range(1, steps):
        sent = None
        if t > 1:
            sent = lax.ppermute(known, "row", hop_z_early(t))
        last = lax.ppermute(fresh, "row", hop_z(t))
        if t > 1:
            acc = early(sc, base, sent, blocks0)
        if t == 7:
            rows_a = collect(sc, range(4), own_a, {**before, 7: [sent]}, back)
            acc, rows_a = lax.optimization_barrier((acc, rows_a))
            pieces_a = spread_y(rows_a)
        fresh = step(t, sc, acc, last, inverse[t], blocks0)
        own_s = jnp.where(z == t, fresh, own_s)
        before[t] = [last] if t == 1 else [sent, last]
        known = last[None] if t == 1 else jnp.concatenate([sent, last[None]])
        if t == 3:
            fresh, left1, right1 = lax.optimization_barrier((fresh, left1, right1))
            near1, far1, near_other1 = rest_of_x(panel1, left1, right1)
        if t == 4:
            first_half = after(own_s, fresh)
            back = [
                lax.ppermute(first_half, "row", back_z(d, range(1, 4))) for d in (1, 2, 3)
            ]
        if t == 5:
            fresh, far1, near1, near_other1, *back = lax.optimization_barrier(
                (fresh, far1, near1, near_other1, *back)
            )
            far_other1 = lax.ppermute(far1, "col", SWAP)
            own_a = own_s
    blocks1 = [in_vmem(v) for v in (near1, far1, near_other1, far_other1)]

    out_s, rest = final(0, sc, steps, pieces_a, blocks0, blocks1, rhs)
    back = [lax.ppermute(own_s, "row", back_z(d, range(4, 8))) for d in range(1, 8)]
    rows_b = collect(sc, range(4, 8), own_s, before, back)
    rows_b = after(rows_b, pieces_a[2], pieces_a[3])
    pieces_b = spread_y(rows_b)
    return tuple(final(4, sc, steps, pieces_b, blocks0, blocks1, rest, out_s))


def solution(mesh):
    placed = (P(None, "row", None, "col", None), P(None, "row", None, "col"), P())
    return jax.shard_map(
        on_device,
        mesh=mesh,
        in_specs=placed,
        out_specs=(P(None, None, "col"), P(None, "row", None, "col")),
        check_vma=False,
    )
```

```python
import jax
import jax.numpy as jnp
from jax import lax
from jax.experimental import pallas as pl
from jax.experimental.pallas import tpu as pltpu
from jax.sharding import PartitionSpec as P


NY, NZ, NX = 4, 8, 4
NT = (((1,), (1,)), ((), ()))
BF = jnp.bfloat16
F32 = jnp.float32


def row_of(y, z):
    return (y % NY) * NZ + z % NZ


def shift_y(d):
    return [(row_of(y, z), row_of(y + d, z)) for y in range(NY) for z in range(NZ)]


def from_plane(y, to):
    return [(row_of(y, z), row_of(to, z)) for z in range(NZ)]


def back_z(d, rows):
    return [(row_of(y, k), row_of(y, k - d)) for y in range(NY) for k in rows if k >= d]


def hop_z(t):
    return [(row_of(y, t - 1), row_of(y, t)) for y in range(NY)]


def hop_z_early(t):
    return hop_z(t) + [(row_of(0, t + 3), row_of(0, t + 4))]


def shift_x(d):
    n = 2 * NX
    return [(i, (i + 2 * d) % n) for i in range(n)]


SWAP = [(i, i ^ 1) for i in range(2 * NX)]


def after(x, *deps):
    return lax.optimization_barrier((x, *deps))[0]


VMEM = pl.BlockSpec(memory_space=pltpu.VMEM)
SMEM = pl.BlockSpec(memory_space=pltpu.SMEM)
LIMIT = 8 * 1024 * 1024
PLACE, KIND, ROWS, AT_Z, PLANE = 0, 8, 16, 17, 18


def params(limit=LIMIT):
    return pltpu.CompilerParams(vmem_limit_bytes=limit)


def times_block(sc, j, low, blocks, use, flip=False):
    place = sc[PLACE + j]
    for kind, ref in enumerate(blocks):

        @pl.when(sc[KIND + j] == kind)
        def _():
            block = ref[place] if len(ref.shape) == 3 else ref[...]
            pair = (block, low) if flip else (low, block)
            use(lax.dot_general(*pair, NT, preferred_element_type=F32))


def early_kernel(sc, base, solved, *refs):
    *blocks, out = refs
    out[...] = base[...].astype(F32)

    def subtract(value):
        out[...] -= value

    @pl.loop(0, solved.shape[0])
    def _(j):
        times_block(sc, j, solved[j], blocks, subtract)


def early(sc, base, solved, blocks):
    n = solved.shape[0]
    c, b = base.shape
    return pl.pallas_call(
        early_kernel,
        out_shape=jax.ShapeDtypeStruct((c, b), F32),
        in_specs=[SMEM] + [VMEM] * (2 + len(blocks)),
        out_specs=VMEM,
        compiler_params=params(),
        cost_estimate=pl.CostEstimate(
            flops=2 * n * c * b * b, bytes_accessed=n * b * b, transcendentals=0
        ),
        name="early",
    )(sc, base, solved, *blocks)


def step_kernel(t, sc, acc, last, inv, *refs):
    *blocks, out, base = refs

    def subtract(value):
        base[...] = (acc[...] - value).astype(BF)

    times_block(sc, t - 1, last[...], blocks, subtract)
    out[...] = lax.dot_general(
        base[...], inv[...], NT, preferred_element_type=F32
    ).astype(BF)


def step(t, sc, acc, last, inv, blocks):
    c, b = acc.shape
    return pl.pallas_call(
        lambda *refs: step_kernel(t, *refs),
        out_shape=jax.ShapeDtypeStruct((c, b), BF),
        in_specs=[SMEM] + [VMEM] * (3 + len(blocks)),
        out_specs=VMEM,
        scratch_shapes=[pltpu.VMEM((c, b), BF)],
        compiler_params=params(),
        cost_estimate=pl.CostEstimate(
            flops=4 * c * b * b, bytes_accessed=2 * b * b, transcendentals=0
        ),
        name="step",
    )(sc, acc, last, inv, *blocks)


def first_kernel(base, inv, out):
    out[...] = lax.dot_general(
        base[...], inv[...], NT, preferred_element_type=F32
    ).astype(BF)


def first(base, inv):
    return pl.pallas_call(
        first_kernel,
        out_shape=jax.ShapeDtypeStruct(base.shape, BF),
        in_specs=[VMEM, VMEM],
        out_specs=VMEM,
        compiler_params=params(),
        name="first",
    )(base, inv)


def hold(parts, stack=False):
    one = parts[0].shape
    shape = (len(parts), *one) if stack else (len(parts) * one[0], *one[1:])

    def kernel(*refs):
        *ins, out = refs
        for i, ref in enumerate(ins):
            if stack:
                out[i] = ref[...]
            else:
                out[i * one[0] : (i + 1) * one[0]] = ref[...]

    return pl.pallas_call(
        kernel,
        out_shape=jax.ShapeDtypeStruct(shape, parts[0].dtype),
        in_specs=[VMEM] * len(parts),
        out_specs=VMEM,
        compiler_params=params(),
        cost_estimate=pl.CostEstimate(
            flops=0, bytes_accessed=4 * len(parts) * one[0] * one[1], transcendentals=0
        ),
        name="hold",
    )(*parts)


def collect(sc, rows, own, before, after_own):
    c, b = own.shape
    names, arrays = {}, []

    def ref_of(x):
        if id(x) not in names:
            names[id(x)] = len(arrays)
            arrays.append(x)
        return names[id(x)]

    def source(z, k):
        if k == z:
            return ref_of(own), None
        if k > z:
            return ref_of(after_own[k - z - 1]), None
        at = 0
        for x in before[z]:
            if len(x.shape) == 2:
                if at == k:
                    return ref_of(x), None
                at += 1
            else:
                if at <= k < at + x.shape[0]:
                    return ref_of(x), k - at
                at += x.shape[0]

    plan = [[source(z, k) for k in rows] for z in range(NZ)]

    def kernel(sc, *refs):
        *ins, out = refs
        for z in range(NZ):

            @pl.when(sc[AT_Z] == z)
            def _():
                for i, (which, at) in enumerate(plan[z]):
                    out[i] = ins[which][...] if at is None else ins[which][at]

    return pl.pallas_call(
        kernel,
        out_shape=jax.ShapeDtypeStruct((len(rows), c, b), BF),
        in_specs=[SMEM] + [VMEM] * len(arrays),
        out_specs=VMEM,
        compiler_params=params(),
        cost_estimate=pl.CostEstimate(
            flops=0, bytes_accessed=4 * len(rows) * c * b, transcendentals=0
        ),
        name="collect",
    )(sc, *arrays)


def spread_y(rows):
    half = rows.shape[0] // 2
    before = lax.ppermute(rows, "row", shift_y(1))
    behind = lax.ppermute(rows, "row", shift_y(-1))
    far_a = lax.ppermute(before[:half], "row", shift_y(1))
    far_b = lax.ppermute(behind[half:], "row", shift_y(-1))
    return rows, behind, far_a, far_b, before


def final_kernel(start, sc, every, behind, far_a, far_b, before, *refs):
    blocks0, blocks1, rest = refs[:4], refs[4:8], refs[8:]
    rhs, (out_s, out_r, low, eye) = rest[0], rest[-4:]
    i = pl.program_id(0)
    c = every.shape[1]
    half = far_a.shape[0]
    split = half < every.shape[0]

    @pl.when(i == 0)
    def _():
        out_r[...] = rhs[...]
        across = lax.broadcasted_iota(jnp.int32, eye.shape, 0)
        down = lax.broadcasted_iota(jnp.int32, eye.shape, 1)
        eye[...] = (across == down).astype(F32).astype(BF)

    def put(m, value):
        low[pl.ds(pl.multiple_of(sc[PLANE + m] * c, c), c), :] = value

    put(0, every[i])
    put(1, behind[i])
    put(3, before[i])

    @pl.when(i < half)
    def _():
        put(2, far_a[i])

    if split:

        @pl.when(i >= half)
        def _():
            put(2, far_b[i - half])

    solved = low[...]
    out_s[0] = lax.dot_general(eye[...], solved, NT, preferred_element_type=F32)

    def remove(q):
        def use(value):
            out_r[q, 0] -= value

        return use

    k = start + i
    times_block(sc, k, solved, blocks1, remove(1), flip=True)

    @pl.when(k < sc[ROWS])
    def _():
        times_block(sc, k, solved, blocks0, remove(0), flip=True)


def final(start, sc, steps, pieces, blocks0, blocks1, rhs, out_s=None):
    n, c, b = pieces[0].shape
    cols = rhs.shape[3]
    args = [sc, *pieces, *blocks0, *blocks1, rhs]
    specs = [SMEM] + [VMEM] * (len(args) - 1)
    alias = {}
    if out_s is not None:
        alias = {len(args): 0}
        args.append(out_s)
        specs.append(pl.BlockSpec(memory_space=pl.ANY))
    return pl.pallas_call(
        lambda *refs: final_kernel(start, *refs),
        out_shape=(
            jax.ShapeDtypeStruct((steps, b, cols), F32),
            jax.ShapeDtypeStruct(rhs.shape, F32),
        ),
        grid=(n,),
        in_specs=specs,
        out_specs=(
            pl.BlockSpec((1, b, cols), lambda i: (start + i, 0, 0)),
            pl.BlockSpec(rhs.shape, lambda i: (0, 0, 0, 0)),
        ),
        scratch_shapes=[pltpu.VMEM((cols, b), BF), pltpu.VMEM((b, b), BF)],
        input_output_aliases=alias,
        compiler_params=params(2 * LIMIT),
        cost_estimate=pl.CostEstimate(
            flops=6 * n * b * b * cols,
            bytes_accessed=4 * n * b * cols,
            transcendentals=0,
        ),
        name="final",
    )(*args)


def on_device(panel, rhs, inverse):
    steps = inverse.shape[0]
    block = panel.shape[2]
    quarter = rhs.shape[3] // NY
    half = block // 2
    row = lax.axis_index("row")
    col = lax.axis_index("col")
    y, z = row // NZ, row % NZ
    x, core = col // 2, col % 2

    j = jnp.arange(steps, dtype=jnp.int32)
    away = (j // 2 - x) % NX
    place = jnp.where(away == 3, 1, jnp.where(away == 1, 2, 0))
    kind = (away == 2) + 2 * (j % 2 != core)
    limit = jnp.where(y == NY - 1, z, 0)
    plane = (jnp.arange(NY, dtype=jnp.int32) + y) % NY
    sc = jnp.concatenate(
        [place, kind.astype(jnp.int32), limit[None], z[None], plane]
    ).astype(jnp.int32)

    panel0 = panel[0, 0, :, 0, :]
    top, low = panel0[:half], panel0[half:]
    up_a = lax.ppermute(top, "row", from_plane(3, 0))
    down_b = lax.ppermute(low, "row", from_plane(3, 2))
    up_b = lax.ppermute(low, "row", from_plane(3, 0) + [(row_of(1, 0), row_of(2, 0))])
    down_a = lax.ppermute(top, "row", from_plane(3, 2) + [(row_of(0, 0), row_of(1, 0))])
    far_a = lax.ppermute(up_a, "row", from_plane(0, 1))
    far_b = lax.ppermute(down_b, "row", from_plane(2, 1))

    def by_plane(at0, at1, at2, at3):
        return jnp.where(
            y == 3, at3, jnp.where(y == 0, at0, jnp.where(y == 2, at2, at1))
        )

    window = jnp.concatenate(
        [by_plane(up_a, far_a, down_a, top), by_plane(up_b, far_b, down_b, low)]
    )

    panel1 = panel[1, 0, :, 0, :]
    left1 = lax.ppermute(panel1, "col", shift_x(1))
    right1 = lax.ppermute(panel1, "col", shift_x(-1))
    window, left1, right1 = lax.optimization_barrier((window, left1, right1))

    left = lax.ppermute(window, "col", shift_x(1))
    right = lax.ppermute(window, "col", shift_x(-1))
    zt = rhs[0, 0].astype(BF).T
    zq = [zt[i * quarter : (i + 1) * quarter] for i in range(NY)]
    ready = [after(zq[0], up_a), after(zq[1], far_a), after(zq[2], down_b)]
    zr = [lax.ppermute(ready[i], "row", from_plane(3, i)) for i in range(NY - 1)]
    near1 = hold([panel1, left1, right1], stack=True)
    near_other1 = lax.ppermute(near1, "col", SWAP)
    left, right, near_other1, left1, right1, *zr = lax.optimization_barrier(
        (left, right, near_other1, left1[:half], right1[half:], *zr)
    )
    base = by_plane(*zr, zq[3])
    far_a = lax.ppermute(left[:half], "col", shift_x(1))
    far_b = lax.ppermute(right[half:], "col", shift_x(-1))
    near = jnp.stack([window, left, right])
    near_other = lax.ppermute(near, "col", SWAP)
    far_a, far_b, near_other = lax.optimization_barrier((far_a, far_b, near_other))
    far = hold([far_a, far_b])
    far_other = hold([lax.ppermute(far, "col", SWAP)])
    blocks0 = [near, far, near_other, far_other]

    fresh = first(base, inverse[0])
    own_s = fresh
    acc = base.astype(F32)
    known = None
    before = {0: []}
    for t in range(1, steps):
        sent = None
        if t > 1:
            sent = lax.ppermute(known, "row", hop_z_early(t))
        last = lax.ppermute(fresh, "row", hop_z(t))
        if t > 1:
            acc = early(sc, base, after(sent, fresh), blocks0)
        if t == 2:
            left1, right1 = after(left1, acc), after(right1, acc)
            far1 = [
                lax.ppermute(left1, "col", shift_x(1)),
                lax.ppermute(right1, "col", shift_x(-1)),
            ]
        fresh = step(t, sc, acc, last, inverse[t], blocks0)
        own_s = jnp.where(z == t, fresh, own_s)
        before[t] = [last] if t == 1 else [sent, last]
        known = last[None] if t == 1 else jnp.concatenate([sent, last[None]])

    far1 = hold([after(far1[0], fresh), far1[1]])
    far_other1 = lax.ppermute(far1, "col", SWAP)
    blocks1 = [near1, far1, near_other1, far_other1]
    back = [
        lax.ppermute(own_s, "row", back_z(d, range(1 if d < 4 else 4, 8)))
        for d in range(1, 8)
    ]
    rows_a = collect(sc, range(4), own_s, before, back)
    before_a = lax.ppermute(rows_a, "row", shift_y(1))
    behind_a = lax.ppermute(rows_a, "row", shift_y(-1))
    far_a = lax.ppermute(rows_a, "row", shift_y(2))
    pieces_a = (rows_a, behind_a, far_a, far_a, before_a)
    out_s, rest = final(0, sc, steps, pieces_a, blocks0, blocks1, rhs)
    rows_b = collect(sc, range(4, 8), own_s, before, back)
    rows_b = after(rows_b, before_a, behind_a)
    pieces_b = spread_y(rows_b)
    return tuple(final(4, sc, steps, pieces_b, blocks0, blocks1, rest, out_s))


def solution(mesh):
    placed = (P(None, "row", None, "col", None), P(None, "row", None, "col"), P())
    return jax.shard_map(
        on_device,
        mesh=mesh,
        in_specs=placed,
        out_specs=(P(None, None, "col"), P(None, "row", None, "col")),
        check_vma=False,
    )
```

```python
import jax
import jax.numpy as jnp
from jax import lax
from jax.experimental import pallas as pl
from jax.experimental.pallas import tpu as pltpu
from jax.sharding import PartitionSpec as P


NY, NZ, NX = 4, 8, 4
NT = (((1,), (1,)), ((), ()))
BF = jnp.bfloat16
F32 = jnp.float32


def row_of(y, z):
    return (y % NY) * NZ + z % NZ


def shift_y(d):
    return [(row_of(y, z), row_of(y + d, z)) for y in range(NY) for z in range(NZ)]


def from_plane(y, to):
    return [(row_of(y, z), row_of(to, z)) for z in range(NZ)]


def back_z(d, rows):
    return [(row_of(y, k), row_of(y, k - d)) for y in range(NY) for k in rows if k >= d]


def hop_z(t):
    return [(row_of(y, t - 1), row_of(y, t)) for y in range(NY)]


def hop_z_early(t):
    return hop_z(t) + [(row_of(0, t + 3), row_of(0, t + 4))]


def shift_x(d):
    n = 2 * NX
    return [(i, (i + 2 * d) % n) for i in range(n)]


SWAP = [(i, i ^ 1) for i in range(2 * NX)]


def after(x, *deps):
    return lax.optimization_barrier((x, *deps))[0]


VMEM = pl.BlockSpec(memory_space=pltpu.VMEM)
SMEM = pl.BlockSpec(memory_space=pltpu.SMEM)
LIMIT = 8 * 1024 * 1024
PLACE, KIND, ROWS, AT_Z, PLANE = 0, 8, 16, 17, 18


def params(limit=LIMIT):
    return pltpu.CompilerParams(vmem_limit_bytes=limit)


def times_block(sc, j, low, blocks, use, flip=False):
    place = sc[PLACE + j]
    for kind, ref in enumerate(blocks):

        @pl.when(sc[KIND + j] == kind)
        def _():
            block = ref[place] if len(ref.shape) == 3 else ref[...]
            pair = (block, low) if flip else (low, block)
            use(lax.dot_general(*pair, NT, preferred_element_type=F32))


def early_kernel(sc, base, solved, *refs):
    *blocks, out = refs
    out[...] = base[...].astype(F32)

    def subtract(value):
        out[...] -= value

    @pl.loop(0, solved.shape[0])
    def _(j):
        times_block(sc, j, solved[j], blocks, subtract)


def early(sc, base, solved, blocks):
    n = solved.shape[0]
    c, b = base.shape
    return pl.pallas_call(
        early_kernel,
        out_shape=jax.ShapeDtypeStruct((c, b), F32),
        in_specs=[SMEM] + [VMEM] * (2 + len(blocks)),
        out_specs=VMEM,
        compiler_params=params(),
        cost_estimate=pl.CostEstimate(
            flops=2 * n * c * b * b, bytes_accessed=n * b * b, transcendentals=0
        ),
        name="early",
    )(sc, base, solved, *blocks)


def step_kernel(t, sc, acc, last, inv, *refs):
    *blocks, out, base = refs

    def subtract(value):
        base[...] = (acc[...] - value).astype(BF)

    times_block(sc, t - 1, last[...], blocks, subtract)
    out[...] = lax.dot_general(
        base[...], inv[t], NT, preferred_element_type=F32
    ).astype(BF)


def step(t, sc, acc, last, inv, blocks):
    c, b = acc.shape
    return pl.pallas_call(
        lambda *refs: step_kernel(t, *refs),
        out_shape=jax.ShapeDtypeStruct((c, b), BF),
        in_specs=[SMEM] + [VMEM] * (3 + len(blocks)),
        out_specs=VMEM,
        scratch_shapes=[pltpu.VMEM((c, b), BF)],
        compiler_params=params(),
        cost_estimate=pl.CostEstimate(
            flops=4 * c * b * b, bytes_accessed=2 * b * b, transcendentals=0
        ),
        name="step",
    )(sc, acc, last, inv, *blocks)


def first_kernel(base, inv, out):
    out[...] = lax.dot_general(
        base[...], inv[0], NT, preferred_element_type=F32
    ).astype(BF)


def first(base, inv):
    return pl.pallas_call(
        first_kernel,
        out_shape=jax.ShapeDtypeStruct(base.shape, BF),
        in_specs=[VMEM, VMEM],
        out_specs=VMEM,
        compiler_params=params(),
        name="first",
    )(base, inv)


def hold(parts, stack=False):
    one = parts[0].shape
    shape = (len(parts), *one) if stack else (len(parts) * one[0], *one[1:])

    def kernel(*refs):
        *ins, out = refs
        for i, ref in enumerate(ins):
            if stack:
                out[i] = ref[...]
            else:
                out[i * one[0] : (i + 1) * one[0]] = ref[...]

    return pl.pallas_call(
        kernel,
        out_shape=jax.ShapeDtypeStruct(shape, parts[0].dtype),
        in_specs=[VMEM] * len(parts),
        out_specs=VMEM,
        compiler_params=params(),
        cost_estimate=pl.CostEstimate(
            flops=0, bytes_accessed=4 * len(parts) * one[0] * one[1], transcendentals=0
        ),
        name="hold",
    )(*parts)


def collect(sc, rows, own, before, after_own):
    c, b = own.shape
    names, arrays = {}, []

    def ref_of(x):
        if id(x) not in names:
            names[id(x)] = len(arrays)
            arrays.append(x)
        return names[id(x)]

    def source(z, k):
        if k == z:
            return ref_of(own), None
        if k > z:
            return ref_of(after_own[k - z - 1]), None
        at = 0
        for x in before[z]:
            if len(x.shape) == 2:
                if at == k:
                    return ref_of(x), None
                at += 1
            else:
                if at <= k < at + x.shape[0]:
                    return ref_of(x), k - at
                at += x.shape[0]

    plan = [[source(z, k) for k in rows] for z in range(NZ)]

    def kernel(sc, *refs):
        *ins, out = refs
        for z in range(NZ):

            @pl.when(sc[AT_Z] == z)
            def _():
                for i, (which, at) in enumerate(plan[z]):
                    out[i] = ins[which][...] if at is None else ins[which][at]

    return pl.pallas_call(
        kernel,
        out_shape=jax.ShapeDtypeStruct((len(rows), c, b), BF),
        in_specs=[SMEM] + [VMEM] * len(arrays),
        out_specs=VMEM,
        compiler_params=params(),
        cost_estimate=pl.CostEstimate(
            flops=0, bytes_accessed=4 * len(rows) * c * b, transcendentals=0
        ),
        name="collect",
    )(sc, *arrays)


def spread_y(rows):
    half = rows.shape[0] // 2
    before = lax.ppermute(rows, "row", shift_y(1))
    behind = lax.ppermute(rows, "row", shift_y(-1))
    far_a = lax.ppermute(before[:half], "row", shift_y(1))
    far_b = lax.ppermute(behind[half:], "row", shift_y(-1))
    return rows, behind, far_a, far_b, before


def final_kernel(start, sc, every, behind, far_a, far_b, before, *refs):
    blocks0, blocks1, rest = refs[:4], refs[4:8], refs[8:]
    rhs, (out_s, out_r, low, eye) = rest[0], rest[-4:]
    i = pl.program_id(0)
    c = every.shape[1]
    half = far_a.shape[0]
    split = half < every.shape[0]

    @pl.when(i == 0)
    def _():
        out_r[...] = rhs[...]
        across = lax.broadcasted_iota(jnp.int32, eye.shape, 0)
        down = lax.broadcasted_iota(jnp.int32, eye.shape, 1)
        eye[...] = (across == down).astype(F32).astype(BF)

    def put(m, value):
        low[pl.ds(pl.multiple_of(sc[PLANE + m] * c, c), c), :] = value

    put(0, every[i])
    put(1, behind[i])
    put(3, before[i])

    @pl.when(i < half)
    def _():
        put(2, far_a[i])

    if split:

        @pl.when(i >= half)
        def _():
            put(2, far_b[i - half])

    solved = low[...]
    out_s[0] = lax.dot_general(eye[...], solved, NT, preferred_element_type=F32)

    def remove(q):
        def use(value):
            out_r[q, 0] -= value

        return use

    k = start + i
    times_block(sc, k, solved, blocks1, remove(1), flip=True)

    @pl.when(k < sc[ROWS])
    def _():
        times_block(sc, k, solved, blocks0, remove(0), flip=True)


def final(start, sc, steps, pieces, blocks0, blocks1, rhs, out_s=None):
    n, _, b = pieces[0].shape
    cols = rhs.shape[3]
    args = [sc, *pieces, *blocks0, *blocks1, rhs]
    specs = [SMEM] + [VMEM] * (len(args) - 1)
    alias = {}
    if out_s is not None:
        alias = {len(args): 0}
        args.append(out_s)
        specs.append(pl.BlockSpec(memory_space=pl.ANY))
    return pl.pallas_call(
        lambda *refs: final_kernel(start, *refs),
        out_shape=(
            jax.ShapeDtypeStruct((steps, b, cols), F32),
            jax.ShapeDtypeStruct(rhs.shape, F32),
        ),
        grid=(n,),
        in_specs=specs,
        out_specs=(
            pl.BlockSpec((1, b, cols), lambda i: (start + i, 0, 0)),
            pl.BlockSpec(rhs.shape, lambda i: (0, 0, 0, 0)),
        ),
        scratch_shapes=[pltpu.VMEM((cols, b), BF), pltpu.VMEM((b, b), BF)],
        input_output_aliases=alias,
        compiler_params=params(2 * LIMIT),
        cost_estimate=pl.CostEstimate(
            flops=6 * n * b * b * cols,
            bytes_accessed=4 * n * b * cols,
            transcendentals=0,
        ),
        name="final",
    )(*args)


def on_device(panel, rhs, inverse):
    steps = inverse.shape[0]
    block = panel.shape[2]
    quarter = rhs.shape[3] // NY
    half = block // 2
    row = lax.axis_index("row")
    col = lax.axis_index("col")
    y, z = row // NZ, row % NZ
    x, core = col // 2, col % 2

    j = jnp.arange(steps, dtype=jnp.int32)
    away = (j // 2 - x) % NX
    place = jnp.where(away == 3, 1, jnp.where(away == 1, 2, 0))
    kind = (away == 2) + 2 * (j % 2 != core)
    limit = jnp.where(y == NY - 1, z, 0)
    plane = (jnp.arange(NY, dtype=jnp.int32) + y) % NY
    sc = jnp.concatenate(
        [place, kind.astype(jnp.int32), limit[None], z[None], plane]
    ).astype(jnp.int32)

    panel0 = panel[0, 0, :, 0, :]
    top, low = panel0[:half], panel0[half:]
    up_a = lax.ppermute(top, "row", from_plane(3, 0))
    down_b = lax.ppermute(low, "row", from_plane(3, 2))
    up_b = lax.ppermute(low, "row", from_plane(3, 0) + [(row_of(1, 0), row_of(2, 0))])
    down_a = lax.ppermute(top, "row", from_plane(3, 2) + [(row_of(0, 0), row_of(1, 0))])
    far_a = lax.ppermute(up_a, "row", from_plane(0, 1))
    far_b = lax.ppermute(down_b, "row", from_plane(2, 1))

    def by_plane(at0, at1, at2, at3):
        return jnp.where(
            y == 3, at3, jnp.where(y == 0, at0, jnp.where(y == 2, at2, at1))
        )

    window = jnp.concatenate(
        [by_plane(up_a, far_a, down_a, top), by_plane(up_b, far_b, down_b, low)]
    )

    panel1 = panel[1, 0, :, 0, :]
    left1 = lax.ppermute(panel1, "col", shift_x(1))
    right1 = lax.ppermute(panel1, "col", shift_x(-1))
    window, left1, right1 = lax.optimization_barrier((window, left1, right1))

    left = lax.ppermute(window, "col", shift_x(1))
    right = lax.ppermute(window, "col", shift_x(-1))
    zt = rhs[0, 0].astype(BF).T
    zq = [zt[i * quarter : (i + 1) * quarter] for i in range(NY)]
    ready = [after(zq[0], up_a), after(zq[1], far_a), after(zq[2], down_b)]
    zr = [lax.ppermute(ready[i], "row", from_plane(3, i)) for i in range(NY - 1)]
    near1 = hold([after(panel1, zr[0]), left1, right1], stack=True)
    near_other1 = lax.ppermute(near1, "col", SWAP)
    inverse = hold([inverse])
    left, right, near_other1, left1, right1, inverse, *zr = lax.optimization_barrier(
        (left, right, near_other1, left1[:half], right1[half:], inverse, *zr)
    )
    base = by_plane(*zr, zq[3])
    far_a, far_b = left[:half], right[half:]
    near = jnp.stack([after(window, far_a, far_b), left, right])
    far_a = lax.ppermute(far_a, "col", shift_x(1))
    far_b = lax.ppermute(far_b, "col", shift_x(-1))
    near_other = lax.ppermute(near, "col", SWAP)
    far_a, far_b, near_other = lax.optimization_barrier((far_a, far_b, near_other))
    far = hold([far_a, far_b])
    far_other = hold([lax.ppermute(far, "col", SWAP)])
    blocks0 = [near, far, near_other, far_other]

    fresh = first(base, inverse)
    own_s = fresh
    acc = base.astype(F32)
    known = None
    before = {0: []}
    for t in range(1, steps):
        sent = None
        if t > 1:
            sent = lax.ppermute(known, "row", hop_z_early(t))
        last = lax.ppermute(fresh, "row", hop_z(t))
        if t > 1:
            acc = early(sc, base, after(sent, fresh), blocks0)
            last = after(last, acc)
        if t == 2:
            left1, right1 = after(left1, acc), after(right1, acc)
            far1 = [
                lax.ppermute(left1, "col", shift_x(1)),
                lax.ppermute(right1, "col", shift_x(-1)),
            ]
        fresh = step(t, sc, acc, last, inverse, blocks0)
        own_s = jnp.where(z == t, fresh, own_s)
        before[t] = [last] if t == 1 else [sent, last]
        known = last[None] if t == 1 else jnp.concatenate([sent, last[None]])

    far1 = hold([after(far1[0], fresh), far1[1]])
    far_other1 = lax.ppermute(far1, "col", SWAP)
    blocks1 = [near1, far1, near_other1, far_other1]
    back = [
        lax.ppermute(own_s, "row", back_z(d, range(1 if d < 4 else 4, 8)))
        for d in range(1, 8)
    ]
    rows_a = collect(sc, range(4), own_s, before, back)
    before_a = lax.ppermute(rows_a, "row", shift_y(1))
    behind_a = lax.ppermute(rows_a, "row", shift_y(-1))
    far_a = lax.ppermute(rows_a, "row", shift_y(2))
    pieces_a = (rows_a, behind_a, far_a, far_a, before_a)
    out_s, rest = final(0, sc, steps, pieces_a, blocks0, blocks1, rhs)
    rows_b = collect(sc, range(4, 8), own_s, before, back)
    rows_b = after(rows_b, before_a, behind_a)
    pieces_b = spread_y(rows_b)
    return tuple(final(4, sc, steps, pieces_b, blocks0, blocks1, rest, out_s))


def solution(mesh):
    placed = (P(None, "row", None, "col", None), P(None, "row", None, "col"), P())
    return jax.shard_map(
        on_device,
        mesh=mesh,
        in_specs=placed,
        out_specs=(P(None, None, "col"), P(None, "row", None, "col")),
        check_vma=False,
    )
```

```python
import jax
import jax.numpy as jnp
from jax import lax
from jax.experimental import pallas as pl
from jax.experimental.pallas import tpu as pltpu
from jax.sharding import PartitionSpec as P


NY, NZ, NX = 4, 8, 4
NT = (((1,), (1,)), ((), ()))
BF = jnp.bfloat16
F32 = jnp.float32


def row_of(y, z):
    return (y % NY) * NZ + z % NZ


def shift_y(d):
    return [(row_of(y, z), row_of(y + d, z)) for y in range(NY) for z in range(NZ)]


def from_plane(y, to):
    return [(row_of(y, z), row_of(to, z)) for z in range(NZ)]


def back_z(d, rows):
    return [(row_of(y, k), row_of(y, k - d)) for y in range(NY) for k in rows if k >= d]


def hop_z(t):
    return [(row_of(y, t - 1), row_of(y, t)) for y in range(NY)]


def hop_z_early(t):
    return hop_z(t) + [(row_of(0, t + 3), row_of(0, t + 4))]


def shift_x(d):
    n = 2 * NX
    return [(i, (i + 2 * d) % n) for i in range(n)]


SWAP = [(i, i ^ 1) for i in range(2 * NX)]


def after(x, *deps):
    return lax.optimization_barrier((x, *deps))[0]


VMEM = pl.BlockSpec(memory_space=pltpu.VMEM)
SMEM = pl.BlockSpec(memory_space=pltpu.SMEM)
ANY = pl.BlockSpec(memory_space=pl.ANY)
LIMIT = 8 * 1024 * 1024
PLACE, KIND, ROWS, AT_Z, PLANE = 0, 8, 16, 17, 18


def params(limit=LIMIT):
    return pltpu.CompilerParams(vmem_limit_bytes=limit)


def times_block(sc, j, low, blocks, use, flip=False):
    place = sc[PLACE + j]
    for kind, ref in enumerate(blocks):

        @pl.when(sc[KIND + j] == kind)
        def _():
            block = ref[place] if len(ref.shape) == 3 else ref[...]
            pair = (block, low) if flip else (low, block)
            use(lax.dot_general(*pair, NT, preferred_element_type=F32))


def early_kernel(t, sc, base, solved, inverse, *refs):
    *blocks, out, inv, sem = refs
    fetch = pltpu.make_async_copy(inverse.at[t], inv, sem)
    fetch.start()
    out[...] = base[...].astype(F32)

    def subtract(value):
        out[...] -= value

    @pl.loop(0, solved.shape[0])
    def _(j):
        times_block(sc, j, solved[j], blocks, subtract)

    fetch.wait()


def early(t, sc, base, solved, inverse, blocks):
    n = solved.shape[0]
    c, b = base.shape
    return pl.pallas_call(
        lambda *refs: early_kernel(t, *refs),
        out_shape=(
            jax.ShapeDtypeStruct((c, b), F32),
            jax.ShapeDtypeStruct((b, b), BF),
        ),
        in_specs=[SMEM, VMEM, VMEM, ANY] + [VMEM] * len(blocks),
        out_specs=(VMEM, VMEM),
        scratch_shapes=[pltpu.SemaphoreType.DMA],
        compiler_params=params(),
        cost_estimate=pl.CostEstimate(
            flops=2 * n * c * b * b, bytes_accessed=n * b * b, transcendentals=0
        ),
        name="early",
    )(sc, base, solved, inverse, *blocks)


def step_kernel(t, sc, acc, last, inv, *refs):
    *blocks, out, base = refs

    def subtract(value):
        base[...] = (acc[...] - value).astype(BF)

    times_block(sc, t - 1, last[...], blocks, subtract)
    out[...] = lax.dot_general(
        base[...], inv[...], NT, preferred_element_type=F32
    ).astype(BF)


def step(t, sc, acc, last, inv, blocks):
    c, b = acc.shape
    return pl.pallas_call(
        lambda *refs: step_kernel(t, *refs),
        out_shape=jax.ShapeDtypeStruct((c, b), BF),
        in_specs=[SMEM] + [VMEM] * (3 + len(blocks)),
        out_specs=VMEM,
        scratch_shapes=[pltpu.VMEM((c, b), BF)],
        compiler_params=params(),
        cost_estimate=pl.CostEstimate(
            flops=4 * c * b * b, bytes_accessed=2 * b * b, transcendentals=0
        ),
        name="step",
    )(sc, acc, last, inv, *blocks)


def first_kernel(base, inverse, out, inv, here, sems):
    own = pltpu.make_async_copy(inverse.at[0], here, sems.at[0])
    following = pltpu.make_async_copy(inverse.at[1], inv, sems.at[1])
    own.start()
    following.start()
    own.wait()
    out[...] = lax.dot_general(
        base[...], here[...], NT, preferred_element_type=F32
    ).astype(BF)
    following.wait()


def first(base, inverse):
    square = inverse.shape[1:]
    return pl.pallas_call(
        first_kernel,
        out_shape=(
            jax.ShapeDtypeStruct(base.shape, BF),
            jax.ShapeDtypeStruct(square, BF),
        ),
        in_specs=[VMEM, ANY],
        out_specs=(VMEM, VMEM),
        scratch_shapes=[pltpu.VMEM(square, BF), pltpu.SemaphoreType.DMA((2,))],
        compiler_params=params(),
        name="first",
    )(base, inverse)


def hold(parts, stack=False):
    one = parts[0].shape
    shape = (len(parts), *one) if stack else (len(parts) * one[0], *one[1:])

    def kernel(*refs):
        *ins, out = refs
        for i, ref in enumerate(ins):
            if stack:
                out[i] = ref[...]
            else:
                out[i * one[0] : (i + 1) * one[0]] = ref[...]

    return pl.pallas_call(
        kernel,
        out_shape=jax.ShapeDtypeStruct(shape, parts[0].dtype),
        in_specs=[VMEM] * len(parts),
        out_specs=VMEM,
        compiler_params=params(),
        cost_estimate=pl.CostEstimate(
            flops=0, bytes_accessed=4 * len(parts) * one[0] * one[1], transcendentals=0
        ),
        name="hold",
    )(*parts)


def collect(sc, rows, own, before, after_own):
    c, b = own.shape
    names, arrays = {}, []

    def ref_of(x):
        if id(x) not in names:
            names[id(x)] = len(arrays)
            arrays.append(x)
        return names[id(x)]

    def source(z, k):
        if k == z:
            return ref_of(own), None
        if k > z:
            return ref_of(after_own[k - z - 1]), None
        at = 0
        for x in before[z]:
            if len(x.shape) == 2:
                if at == k:
                    return ref_of(x), None
                at += 1
            else:
                if at <= k < at + x.shape[0]:
                    return ref_of(x), k - at
                at += x.shape[0]

    plan = [[source(z, k) for k in rows] for z in range(NZ)]

    def kernel(sc, *refs):
        *ins, out = refs
        for z in range(NZ):

            @pl.when(sc[AT_Z] == z)
            def _():
                for i, (which, at) in enumerate(plan[z]):
                    out[i] = ins[which][...] if at is None else ins[which][at]

    return pl.pallas_call(
        kernel,
        out_shape=jax.ShapeDtypeStruct((len(rows), c, b), BF),
        in_specs=[SMEM] + [VMEM] * len(arrays),
        out_specs=VMEM,
        compiler_params=params(),
        cost_estimate=pl.CostEstimate(
            flops=0, bytes_accessed=4 * len(rows) * c * b, transcendentals=0
        ),
        name="collect",
    )(sc, *arrays)


def spread_y(rows):
    half = rows.shape[0] // 2
    before = lax.ppermute(rows, "row", shift_y(1))
    behind = lax.ppermute(rows, "row", shift_y(-1))
    far_a = lax.ppermute(before[:half], "row", shift_y(1))
    far_b = lax.ppermute(behind[half:], "row", shift_y(-1))
    return rows, behind, far_a, far_b, before


def final_kernel(start, sc, every, behind, far_a, far_b, before, *refs):
    blocks0, blocks1, rest = refs[:4], refs[4:8], refs[8:]
    rhs, (out_s, out_r, low, eye) = rest[0], rest[-4:]
    i = pl.program_id(0)
    c = every.shape[1]
    half = far_a.shape[0]
    split = half < every.shape[0]

    @pl.when(i == 0)
    def _():
        out_r[...] = rhs[...]
        across = lax.broadcasted_iota(jnp.int32, eye.shape, 0)
        down = lax.broadcasted_iota(jnp.int32, eye.shape, 1)
        eye[...] = (across == down).astype(F32).astype(BF)

    def put(m, value):
        low[pl.ds(pl.multiple_of(sc[PLANE + m] * c, c), c), :] = value

    put(0, every[i])
    put(1, behind[i])
    put(3, before[i])

    @pl.when(i < half)
    def _():
        put(2, far_a[i])

    if split:

        @pl.when(i >= half)
        def _():
            put(2, far_b[i - half])

    solved = low[...]
    out_s[0] = lax.dot_general(eye[...], solved, NT, preferred_element_type=F32)

    def remove(q):
        def use(value):
            out_r[q, 0] -= value

        return use

    k = start + i
    times_block(sc, k, solved, blocks1, remove(1), flip=True)

    @pl.when(k < sc[ROWS])
    def _():
        times_block(sc, k, solved, blocks0, remove(0), flip=True)


def final(start, sc, steps, pieces, blocks0, blocks1, rhs, out_s=None):
    n, _, b = pieces[0].shape
    cols = rhs.shape[3]
    args = [sc, *pieces, *blocks0, *blocks1, rhs]
    specs = [SMEM] + [VMEM] * (len(args) - 1)
    alias = {}
    if out_s is not None:
        alias = {len(args): 0}
        args.append(out_s)
        specs.append(pl.BlockSpec(memory_space=pl.ANY))
    return pl.pallas_call(
        lambda *refs: final_kernel(start, *refs),
        out_shape=(
            jax.ShapeDtypeStruct((steps, b, cols), F32),
            jax.ShapeDtypeStruct(rhs.shape, F32),
        ),
        grid=(n,),
        in_specs=specs,
        out_specs=(
            pl.BlockSpec((1, b, cols), lambda i: (start + i, 0, 0)),
            pl.BlockSpec(rhs.shape, lambda i: (0, 0, 0, 0)),
        ),
        scratch_shapes=[pltpu.VMEM((cols, b), BF), pltpu.VMEM((b, b), BF)],
        input_output_aliases=alias,
        compiler_params=params(2 * LIMIT),
        cost_estimate=pl.CostEstimate(
            flops=6 * n * b * b * cols,
            bytes_accessed=4 * n * b * cols,
            transcendentals=0,
        ),
        name="final",
    )(*args)


def on_device(panel, rhs, inverse):
    steps = inverse.shape[0]
    block = panel.shape[2]
    quarter = rhs.shape[3] // NY
    half = block // 2
    row = lax.axis_index("row")
    col = lax.axis_index("col")
    y, z = row // NZ, row % NZ
    x, core = col // 2, col % 2

    j = jnp.arange(steps, dtype=jnp.int32)
    away = (j // 2 - x) % NX
    place = jnp.where(away == 3, 1, jnp.where(away == 1, 2, 0))
    kind = (away == 2) + 2 * (j % 2 != core)
    limit = jnp.where(y == NY - 1, z, 0)
    plane = (jnp.arange(NY, dtype=jnp.int32) + y) % NY
    sc = jnp.concatenate(
        [place, kind.astype(jnp.int32), limit[None], z[None], plane]
    ).astype(jnp.int32)

    panel0 = panel[0, 0, :, 0, :]
    top, low = panel0[:half], panel0[half:]
    up_a = lax.ppermute(top, "row", from_plane(3, 0))
    down_b = lax.ppermute(low, "row", from_plane(3, 2))
    up_b = lax.ppermute(low, "row", from_plane(3, 0) + [(row_of(1, 0), row_of(2, 0))])
    down_a = lax.ppermute(top, "row", from_plane(3, 2) + [(row_of(0, 0), row_of(1, 0))])
    far_a = lax.ppermute(up_a, "row", from_plane(0, 1))
    far_b = lax.ppermute(down_b, "row", from_plane(2, 1))

    def by_plane(at0, at1, at2, at3):
        return jnp.where(
            y == 3, at3, jnp.where(y == 0, at0, jnp.where(y == 2, at2, at1))
        )

    window = jnp.concatenate(
        [by_plane(up_a, far_a, down_a, top), by_plane(up_b, far_b, down_b, low)]
    )

    panel1 = panel[1, 0, :, 0, :]
    left1 = lax.ppermute(panel1, "col", shift_x(1))
    right1 = lax.ppermute(panel1, "col", shift_x(-1))
    window, left1, right1 = lax.optimization_barrier((window, left1, right1))

    left = lax.ppermute(window, "col", shift_x(1))
    right = lax.ppermute(window, "col", shift_x(-1))
    zt = rhs[0, 0].astype(BF).T
    zq = [zt[i * quarter : (i + 1) * quarter] for i in range(NY)]
    ready = [after(zq[0], up_a), after(zq[1], far_a), after(zq[2], down_b)]
    zr = [lax.ppermute(ready[i], "row", from_plane(3, i)) for i in range(NY - 1)]
    near1 = hold([after(panel1, zr[0]), left1, right1], stack=True)
    near_other1 = lax.ppermute(near1, "col", SWAP)
    left, right, near_other1, left1, right1, *zr = lax.optimization_barrier(
        (left, right, near_other1, left1[:half], right1[half:], *zr)
    )
    base = by_plane(*zr, zq[3])
    far_a, far_b = left[:half], right[half:]
    near = jnp.stack([after(window, far_a, far_b), left, right])
    far_a = lax.ppermute(far_a, "col", shift_x(1))
    far_b = lax.ppermute(far_b, "col", shift_x(-1))
    near_other = lax.ppermute(near, "col", SWAP)
    far_a, far_b, near_other = lax.optimization_barrier((far_a, far_b, near_other))
    far = hold([far_a, far_b])
    far_other = hold([lax.ppermute(far, "col", SWAP)])
    blocks0 = [near, far, near_other, far_other]

    fresh, inv = first(base, inverse)
    own_s = fresh
    acc = base.astype(F32)
    known = None
    before = {0: []}
    back_a = []
    for t in range(1, steps):
        sent = None
        if t > 1:
            sent = lax.ppermute(known, "row", hop_z_early(t))
        last = lax.ppermute(fresh, "row", hop_z(t))
        if t > 1:
            acc, inv = early(t, sc, base, after(sent, fresh), inverse, blocks0)
            last = after(last, acc)
        if t == 2:
            left1, right1 = after(left1, acc), after(right1, acc)
            far1 = [
                lax.ppermute(left1, "col", shift_x(1)),
                lax.ppermute(right1, "col", shift_x(-1)),
            ]
        if 4 <= t <= 6:
            back_a.append(
                lax.ppermute((back_a or [own_s])[-1], "row", back_z(1, range(1, 4)))
            )
        if t > 4:
            last = after(last, back_a[t - 5])
        if t == 7:
            rows_a = collect(sc, range(4), own_s, {**before, 7: [sent]}, back_a)
            acc, rows_a = lax.optimization_barrier((acc, rows_a))
            before_a = lax.ppermute(rows_a, "row", shift_y(1))
            behind_a = lax.ppermute(rows_a, "row", shift_y(-1))
            far_a = lax.ppermute(rows_a, "row", shift_y(2))
            pieces_a = (rows_a, behind_a, far_a, far_a, before_a)
        fresh = step(t, sc, acc, last, inv, blocks0)
        own_s = jnp.where(z == t, fresh, own_s)
        before[t] = [last] if t == 1 else [sent, last]
        known = last[None] if t == 1 else jnp.concatenate([sent, last[None]])

    back = [lax.ppermute(own_s, "row", back_z(d, range(4, 8))) for d in range(1, 8)]
    rows_b = collect(sc, range(4, 8), own_s, before, back)
    far1 = hold([after(far1[0], rows_b), far1[1]])
    far_other1 = lax.ppermute(far1, "col", SWAP)
    blocks1 = [near1, far1, near_other1, far_other1]
    out_s, rest = final(0, sc, steps, pieces_a, blocks0, blocks1, rhs)
    rows_b = after(rows_b, before_a, behind_a)
    pieces_b = spread_y(rows_b)
    return tuple(final(4, sc, steps, pieces_b, blocks0, blocks1, rest, out_s))


def solution(mesh):
    placed = (P(None, "row", None, "col", None), P(None, "row", None, "col"), P())
    return jax.shard_map(
        on_device,
        mesh=mesh,
        in_specs=placed,
        out_specs=(P(None, None, "col"), P(None, "row", None, "col")),
        check_vma=False,
    )
```

```python
import jax
import jax.numpy as jnp
from jax import lax
from jax.experimental import pallas as pl
from jax.experimental.pallas import tpu as pltpu
from jax.sharding import PartitionSpec as P


NY, NZ, NX = 4, 8, 4
NT = (((1,), (1,)), ((), ()))
BF = jnp.bfloat16
F32 = jnp.float32


def row_of(y, z):
    return (y % NY) * NZ + z % NZ


def shift_y(d):
    return [(row_of(y, z), row_of(y + d, z)) for y in range(NY) for z in range(NZ)]


def from_plane(y, to):
    return [(row_of(y, z), row_of(to, z)) for z in range(NZ)]


def back_z(d, rows):
    return [(row_of(y, k), row_of(y, k - d)) for y in range(NY) for k in rows if k >= d]


def hop_z(t):
    return [(row_of(y, t - 1), row_of(y, t)) for y in range(NY)]


def hop_z_early(t):
    return hop_z(t) + [(row_of(0, t + 3), row_of(0, t + 4))]


def shift_x(d):
    n = 2 * NX
    return [(i, (i + 2 * d) % n) for i in range(n)]


SWAP = [(i, i ^ 1) for i in range(2 * NX)]


def after(x, *deps):
    return lax.optimization_barrier((x, *deps))[0]


VMEM = pl.BlockSpec(memory_space=pltpu.VMEM)
SMEM = pl.BlockSpec(memory_space=pltpu.SMEM)
ANY = pl.BlockSpec(memory_space=pl.ANY)
HBM = pl.BlockSpec(memory_space=pltpu.HBM)
LIMIT = 8 * 1024 * 1024
PLACE, KIND, ROWS, AT_Z, PLANE = 0, 8, 16, 17, 18


def params(limit=LIMIT):
    return pltpu.CompilerParams(vmem_limit_bytes=limit)


def times_block(sc, j, low, blocks, use, flip=False):
    place = sc[PLACE + j]
    for kind, ref in enumerate(blocks):

        @pl.when(sc[KIND + j] == kind)
        def _():
            block = ref[place] if len(ref.shape) == 3 else ref[...]
            pair = (block, low) if flip else (low, block)
            use(lax.dot_general(*pair, NT, preferred_element_type=F32))


def early_kernel(t, sc, base, solved, inverse, *refs):
    *blocks, out, inv, sem = refs
    fetch = pltpu.make_async_copy(inverse.at[t], inv, sem)
    fetch.start()
    out[...] = base[...].astype(F32)

    def subtract(value):
        out[...] -= value

    @pl.loop(0, solved.shape[0])
    def _(j):
        times_block(sc, j, solved[j], blocks, subtract)

    fetch.wait()


def early(t, sc, base, solved, inverse, blocks):
    n = solved.shape[0]
    c, b = base.shape
    return pl.pallas_call(
        lambda *refs: early_kernel(t, *refs),
        out_shape=(
            jax.ShapeDtypeStruct((c, b), F32),
            jax.ShapeDtypeStruct((b, b), BF),
        ),
        in_specs=[SMEM, VMEM, VMEM, HBM] + [VMEM] * len(blocks),
        out_specs=(VMEM, VMEM),
        scratch_shapes=[pltpu.SemaphoreType.DMA],
        compiler_params=params(),
        cost_estimate=pl.CostEstimate(
            flops=2 * n * c * b * b, bytes_accessed=n * b * b, transcendentals=0
        ),
        name="early",
    )(sc, base, solved, inverse, *blocks)


def step_kernel(t, sc, acc, last, inv, *refs):
    *blocks, out, base = refs

    def subtract(value):
        base[...] = (acc[...] - value).astype(BF)

    times_block(sc, t - 1, last[...], blocks, subtract)
    out[...] = lax.dot_general(
        base[...], inv[...], NT, preferred_element_type=F32
    ).astype(BF)


def step(t, sc, acc, last, inv, blocks):
    c, b = acc.shape
    return pl.pallas_call(
        lambda *refs: step_kernel(t, *refs),
        out_shape=jax.ShapeDtypeStruct((c, b), BF),
        in_specs=[SMEM] + [VMEM] * (3 + len(blocks)),
        out_specs=VMEM,
        scratch_shapes=[pltpu.VMEM((c, b), BF)],
        compiler_params=params(),
        cost_estimate=pl.CostEstimate(
            flops=4 * c * b * b, bytes_accessed=2 * b * b, transcendentals=0
        ),
        name="step",
    )(sc, acc, last, inv, *blocks)


def first_kernel(base, inverse, out, inv, here, sems):
    own = pltpu.make_async_copy(inverse.at[0], here, sems.at[0])
    following = pltpu.make_async_copy(inverse.at[1], inv, sems.at[1])
    own.start()
    following.start()
    own.wait()
    out[...] = lax.dot_general(
        base[...], here[...], NT, preferred_element_type=F32
    ).astype(BF)
    following.wait()


def first(base, inverse):
    square = inverse.shape[1:]
    return pl.pallas_call(
        first_kernel,
        out_shape=(
            jax.ShapeDtypeStruct(base.shape, BF),
            jax.ShapeDtypeStruct(square, BF),
        ),
        in_specs=[VMEM, HBM],
        out_specs=(VMEM, VMEM),
        scratch_shapes=[pltpu.VMEM(square, BF), pltpu.SemaphoreType.DMA((2,))],
        compiler_params=params(),
        name="first",
    )(base, inverse)


def hold(parts, stack=False):
    one = parts[0].shape
    shape = (len(parts), *one) if stack else (len(parts) * one[0], *one[1:])

    def kernel(*refs):
        *ins, out = refs
        for i, ref in enumerate(ins):
            if stack:
                out[i] = ref[...]
            else:
                out[i * one[0] : (i + 1) * one[0]] = ref[...]

    return pl.pallas_call(
        kernel,
        out_shape=jax.ShapeDtypeStruct(shape, parts[0].dtype),
        in_specs=[VMEM] * len(parts),
        out_specs=VMEM,
        compiler_params=params(),
        cost_estimate=pl.CostEstimate(
            flops=0, bytes_accessed=4 * len(parts) * one[0] * one[1], transcendentals=0
        ),
        name="hold",
    )(*parts)


def append(known, last):
    n, c, b = known.shape

    def kernel(known, last, out):
        out[:n] = known[...]
        out[n] = last[...]

    return pl.pallas_call(
        kernel,
        out_shape=jax.ShapeDtypeStruct((n + 1, c, b), BF),
        in_specs=[VMEM, VMEM],
        out_specs=VMEM,
        compiler_params=params(),
        cost_estimate=pl.CostEstimate(
            flops=0, bytes_accessed=4 * (n + 1) * c * b, transcendentals=0
        ),
        name="append",
    )(known, last)


def own_row(sc, solved):
    def kernel(sc, *refs):
        *ins, out = refs
        for z, ref in enumerate(ins):

            @pl.when((sc[AT_Z] == z) if z + 1 < len(ins) else (sc[AT_Z] >= z))
            def _():
                out[...] = ref[...]

    return pl.pallas_call(
        kernel,
        out_shape=jax.ShapeDtypeStruct(solved[0].shape, BF),
        in_specs=[SMEM] + [VMEM] * len(solved),
        out_specs=VMEM,
        compiler_params=params(),
        name="own_row",
    )(sc, *solved)


def collect(sc, rows, own, before, after_own):
    c, b = own.shape
    names, arrays = {}, []

    def ref_of(x):
        if id(x) not in names:
            names[id(x)] = len(arrays)
            arrays.append(x)
        return names[id(x)]

    def source(z, k):
        if k == z:
            return ref_of(own), None
        if k > z:
            return ref_of(after_own[k - z - 1]), None
        at = 0
        for x in before[z]:
            if len(x.shape) == 2:
                if at == k:
                    return ref_of(x), None
                at += 1
            else:
                if at <= k < at + x.shape[0]:
                    return ref_of(x), k - at
                at += x.shape[0]

    plan = [[source(z, k) for k in rows] for z in range(NZ)]

    def kernel(sc, *refs):
        *ins, out = refs
        for z in range(NZ):

            @pl.when(sc[AT_Z] == z)
            def _():
                for i, (which, at) in enumerate(plan[z]):
                    out[i] = ins[which][...] if at is None else ins[which][at]

    return pl.pallas_call(
        kernel,
        out_shape=jax.ShapeDtypeStruct((len(rows), c, b), BF),
        in_specs=[SMEM] + [VMEM] * len(arrays),
        out_specs=VMEM,
        compiler_params=params(),
        cost_estimate=pl.CostEstimate(
            flops=0, bytes_accessed=4 * len(rows) * c * b, transcendentals=0
        ),
        name="collect",
    )(sc, *arrays)


def spread_y(rows):
    half = rows.shape[0] // 2
    before = lax.ppermute(rows, "row", shift_y(1))
    behind = lax.ppermute(rows, "row", shift_y(-1))
    far_a = lax.ppermute(before[:half], "row", shift_y(1))
    far_b = lax.ppermute(behind[half:], "row", shift_y(-1))
    return rows, behind, far_a, far_b, before


def final_kernel(start, sc, every, behind, far_a, far_b, before, *refs):
    blocks0, blocks1, rest = refs[:4], refs[4:8], refs[8:]
    rhs, (out_s, out_r, low, eye) = rest[0], rest[-4:]
    i = pl.program_id(0)
    c = every.shape[1]
    half = far_a.shape[0]
    split = half < every.shape[0]

    @pl.when(i == 0)
    def _():
        out_r[...] = rhs[...]
        across = lax.broadcasted_iota(jnp.int32, eye.shape, 0)
        down = lax.broadcasted_iota(jnp.int32, eye.shape, 1)
        eye[...] = (across == down).astype(F32).astype(BF)

    def put(m, value):
        low[pl.ds(pl.multiple_of(sc[PLANE + m] * c, c), c), :] = value

    put(0, every[i])
    put(1, behind[i])
    put(3, before[i])

    @pl.when(i < half)
    def _():
        put(2, far_a[i])

    if split:

        @pl.when(i >= half)
        def _():
            put(2, far_b[i - half])

    solved = low[...]
    out_s[0] = lax.dot_general(eye[...], solved, NT, preferred_element_type=F32)

    def remove(q):
        def use(value):
            out_r[q, 0] -= value

        return use

    k = start + i
    times_block(sc, k, solved, blocks1, remove(1), flip=True)

    @pl.when(k < sc[ROWS])
    def _():
        times_block(sc, k, solved, blocks0, remove(0), flip=True)


def final(start, sc, steps, pieces, blocks0, blocks1, rhs, out_s=None):
    n, _, b = pieces[0].shape
    cols = rhs.shape[3]
    args = [sc, *pieces, *blocks0, *blocks1, rhs]
    specs = [SMEM] + [VMEM] * (len(args) - 1)
    alias = {}
    if out_s is not None:
        alias = {len(args): 0}
        args.append(out_s)
        specs.append(pl.BlockSpec(memory_space=pl.ANY))
    return pl.pallas_call(
        lambda *refs: final_kernel(start, *refs),
        out_shape=(
            jax.ShapeDtypeStruct((steps, b, cols), F32),
            jax.ShapeDtypeStruct(rhs.shape, F32),
        ),
        grid=(n,),
        in_specs=specs,
        out_specs=(
            pl.BlockSpec((1, b, cols), lambda i: (start + i, 0, 0)),
            pl.BlockSpec(rhs.shape, lambda i: (0, 0, 0, 0)),
        ),
        scratch_shapes=[pltpu.VMEM((cols, b), BF), pltpu.VMEM((b, b), BF)],
        input_output_aliases=alias,
        compiler_params=params(2 * LIMIT),
        cost_estimate=pl.CostEstimate(
            flops=6 * n * b * b * cols,
            bytes_accessed=4 * n * b * cols,
            transcendentals=0,
        ),
        name="final",
    )(*args)


def on_device(panel, rhs, inverse):
    steps = inverse.shape[0]
    block = panel.shape[2]
    quarter = rhs.shape[3] // NY
    half = block // 2
    row = lax.axis_index("row")
    col = lax.axis_index("col")
    y, z = row // NZ, row % NZ
    x, core = col // 2, col % 2

    j = jnp.arange(steps, dtype=jnp.int32)
    away = (j // 2 - x) % NX
    place = jnp.where(away == 3, 1, jnp.where(away == 1, 2, 0))
    kind = (away == 2) + 2 * (j % 2 != core)
    limit = jnp.where(y == NY - 1, z, 0)
    plane = (jnp.arange(NY, dtype=jnp.int32) + y) % NY
    sc = jnp.concatenate(
        [place, kind.astype(jnp.int32), limit[None], z[None], plane]
    ).astype(jnp.int32)

    panel0 = panel[0, 0, :, 0, :]
    top, low = panel0[:half], panel0[half:]
    up_a = lax.ppermute(top, "row", from_plane(3, 0))
    down_b = lax.ppermute(low, "row", from_plane(3, 2))
    up_b = lax.ppermute(low, "row", from_plane(3, 0) + [(row_of(1, 0), row_of(2, 0))])
    down_a = lax.ppermute(top, "row", from_plane(3, 2) + [(row_of(0, 0), row_of(1, 0))])
    far_a = lax.ppermute(up_a, "row", from_plane(0, 1))
    far_b = lax.ppermute(down_b, "row", from_plane(2, 1))

    def by_plane(at0, at1, at2, at3):
        return jnp.where(
            y == 3, at3, jnp.where(y == 0, at0, jnp.where(y == 2, at2, at1))
        )

    window = jnp.concatenate(
        [by_plane(up_a, far_a, down_a, top), by_plane(up_b, far_b, down_b, low)]
    )

    panel1 = panel[1, 0, :, 0, :]
    left1 = lax.ppermute(panel1, "col", shift_x(1))
    right1 = lax.ppermute(panel1, "col", shift_x(-1))
    window, left1, right1 = lax.optimization_barrier((window, left1, right1))

    left = lax.ppermute(window, "col", shift_x(1))
    right = lax.ppermute(window, "col", shift_x(-1))
    zt = rhs[0, 0].astype(BF).T
    zq = [zt[i * quarter : (i + 1) * quarter] for i in range(NY)]
    ready = [after(zq[0], up_a), after(zq[1], far_a), after(zq[2], down_b)]
    zr = [lax.ppermute(ready[i], "row", from_plane(3, i)) for i in range(NY - 1)]
    near1 = hold([after(panel1, zr[0]), left1, right1], stack=True)
    near_other1 = lax.ppermute(near1, "col", SWAP)
    left, right, near_other1, left1, right1, *zr = lax.optimization_barrier(
        (left, right, near_other1, left1[:half], right1[half:], *zr)
    )
    base = by_plane(*zr, zq[3])
    far_a, far_b = left[:half], right[half:]
    near = jnp.stack([after(window, far_a, far_b), left, right])
    far_a = lax.ppermute(far_a, "col", shift_x(1))
    far_b = lax.ppermute(far_b, "col", shift_x(-1))
    near_other = lax.ppermute(near, "col", SWAP)
    far_a, far_b, near_other = lax.optimization_barrier((far_a, far_b, near_other))
    far = hold([far_a, far_b])
    far_other = hold([lax.ppermute(far, "col", SWAP)])
    blocks0 = [near, far, near_other, far_other]

    fresh, inv = first(base, inverse)
    solved = [fresh]
    acc = base.astype(F32)
    known = None
    before = {0: []}
    back_a = []
    for t in range(1, steps):
        sent = None
        if t > 1:
            sent = lax.ppermute(known, "row", hop_z_early(t))
        last = lax.ppermute(fresh, "row", hop_z(t))
        if t > 1:
            acc, inv = early(t, sc, base, after(sent, fresh), inverse, blocks0)
            last = after(last, acc)
        if t == 2:
            left1, right1 = after(left1, acc), after(right1, acc)
            far1 = [
                lax.ppermute(left1, "col", shift_x(1)),
                lax.ppermute(right1, "col", shift_x(-1)),
            ]
        if t == 4:
            own_s = own_row(sc, solved)
        if 4 <= t <= 6:
            back_a.append(
                lax.ppermute((back_a or [own_s])[-1], "row", back_z(1, range(1, 4)))
            )
        if t > 4:
            last = after(last, back_a[t - 5])
        if t == 7:
            rows_a = collect(sc, range(4), own_s, {**before, 7: [sent]}, back_a)
            acc, rows_a = lax.optimization_barrier((acc, rows_a))
            before_a = lax.ppermute(rows_a, "row", shift_y(1))
            behind_a = lax.ppermute(rows_a, "row", shift_y(-1))
            far_a = lax.ppermute(rows_a, "row", shift_y(2))
            pieces_a = (rows_a, behind_a, far_a, far_a, before_a)
        fresh = step(t, sc, acc, last, inv, blocks0)
        solved.append(fresh)
        before[t] = [last] if t == 1 else [sent, last]
        known = last[None] if t == 1 else append(sent, last)

    own_s = own_row(sc, solved)
    back = [lax.ppermute(own_s, "row", back_z(d, range(4, 8))) for d in range(1, 8)]
    rows_b = collect(sc, range(4, 8), own_s, before, back)
    far1 = hold([after(far1[0], rows_b), far1[1]])
    far_other1 = lax.ppermute(far1, "col", SWAP)
    blocks1 = [near1, far1, near_other1, far_other1]
    out_s, rest = final(0, sc, steps, pieces_a, blocks0, blocks1, rhs)
    rows_b = after(rows_b, before_a, behind_a)
    pieces_b = spread_y(rows_b)
    return tuple(final(4, sc, steps, pieces_b, blocks0, blocks1, rest, out_s))


def solution(mesh):
    placed = (P(None, "row", None, "col", None), P(None, "row", None, "col"), P())
    return jax.shard_map(
        on_device,
        mesh=mesh,
        in_specs=placed,
        out_specs=(P(None, None, "col"), P(None, "row", None, "col")),
        check_vma=False,
    )
```

```python
import jax
import jax.numpy as jnp
from jax import lax
from jax.experimental import pallas as pl
from jax.experimental.pallas import tpu as pltpu
from jax.sharding import PartitionSpec as P


NY, NZ, NX = 4, 8, 4
NT = (((1,), (1,)), ((), ()))
BF = jnp.bfloat16
F32 = jnp.float32


def row_of(y, z):
    return (y % NY) * NZ + z % NZ


def shift_y(d):
    return [(row_of(y, z), row_of(y + d, z)) for y in range(NY) for z in range(NZ)]


def from_plane(y, to):
    return [(row_of(y, z), row_of(to, z)) for z in range(NZ)]


def back_z(d, rows):
    return [(row_of(y, k), row_of(y, k - d)) for y in range(NY) for k in rows if k >= d]


def hop_z(t):
    return [(row_of(y, t - 1), row_of(y, t)) for y in range(NY)]


def hop_z_early(t):
    return hop_z(t) + [(row_of(0, t + 3), row_of(0, t + 4))]


def shift_x(d):
    n = 2 * NX
    return [(i, (i + 2 * d) % n) for i in range(n)]


SWAP = [(i, i ^ 1) for i in range(2 * NX)]


def after(x, *deps):
    return lax.optimization_barrier((x, *deps))[0]


VMEM = pl.BlockSpec(memory_space=pltpu.VMEM)
SMEM = pl.BlockSpec(memory_space=pltpu.SMEM)
ANY = pl.BlockSpec(memory_space=pl.ANY)
HBM = pl.BlockSpec(memory_space=pltpu.HBM)
LIMIT = 8 * 1024 * 1024
PLACE, KIND, ROWS, AT_Z, PLANE = 0, 8, 16, 17, 18


def params(limit=LIMIT):
    return pltpu.CompilerParams(vmem_limit_bytes=limit)


def times_block(sc, j, low, blocks, use, flip=False):
    place = sc[PLACE + j]
    for kind, ref in enumerate(blocks):

        @pl.when(sc[KIND + j] == kind)
        def _():
            block = ref[place] if len(ref.shape) == 3 else ref[...]
            pair = (block, low) if flip else (low, block)
            use(lax.dot_general(*pair, NT, preferred_element_type=F32))


def early_kernel(t, sc, base, solved, inverse, *refs):
    *blocks, out, inv, sem = refs

    @pl.when(sc[AT_Z] == t)
    def _():
        fetch = pltpu.make_async_copy(inverse.at[t], inv, sem)
        fetch.start()
        out[...] = base[...].astype(F32)

        def subtract(value):
            out[...] -= value

        @pl.loop(0, solved.shape[0])
        def _(j):
            times_block(sc, j, solved[j], blocks, subtract)

        fetch.wait()


def early(t, sc, base, solved, inverse, blocks):
    n = solved.shape[0]
    c, b = base.shape
    return pl.pallas_call(
        lambda *refs: early_kernel(t, *refs),
        out_shape=(
            jax.ShapeDtypeStruct((c, b), F32),
            jax.ShapeDtypeStruct((b, b), BF),
        ),
        in_specs=[SMEM, VMEM, VMEM, HBM] + [VMEM] * len(blocks),
        out_specs=(VMEM, VMEM),
        scratch_shapes=[pltpu.SemaphoreType.DMA],
        compiler_params=params(),
        cost_estimate=pl.CostEstimate(
            flops=2 * n * c * b * b, bytes_accessed=n * b * b, transcendentals=0
        ),
        name="early",
    )(sc, base, solved, inverse, *blocks)


def step_kernel(t, sc, acc, last, inv, *refs):
    *blocks, out, base = refs

    def subtract(value):
        base[...] = (acc[...] - value).astype(BF)

    @pl.when(sc[AT_Z] == t)
    def _():
        times_block(sc, t - 1, last[...], blocks, subtract)
        out[...] = lax.dot_general(
            base[...], inv[...], NT, preferred_element_type=F32
        ).astype(BF)


def step(t, sc, acc, last, inv, blocks):
    c, b = acc.shape
    return pl.pallas_call(
        lambda *refs: step_kernel(t, *refs),
        out_shape=jax.ShapeDtypeStruct((c, b), BF),
        in_specs=[SMEM] + [VMEM] * (3 + len(blocks)),
        out_specs=VMEM,
        scratch_shapes=[pltpu.VMEM((c, b), BF)],
        compiler_params=params(),
        cost_estimate=pl.CostEstimate(
            flops=4 * c * b * b, bytes_accessed=2 * b * b, transcendentals=0
        ),
        name="step",
    )(sc, acc, last, inv, *blocks)


def first_kernel(base, inverse, out, inv, here, sems):
    own = pltpu.make_async_copy(inverse.at[0], here, sems.at[0])
    following = pltpu.make_async_copy(inverse.at[1], inv, sems.at[1])
    own.start()
    following.start()
    own.wait()
    out[...] = lax.dot_general(
        base[...], here[...], NT, preferred_element_type=F32
    ).astype(BF)
    following.wait()


def first(base, inverse):
    square = inverse.shape[1:]
    return pl.pallas_call(
        first_kernel,
        out_shape=(
            jax.ShapeDtypeStruct(base.shape, BF),
            jax.ShapeDtypeStruct(square, BF),
        ),
        in_specs=[VMEM, HBM],
        out_specs=(VMEM, VMEM),
        scratch_shapes=[pltpu.VMEM(square, BF), pltpu.SemaphoreType.DMA((2,))],
        compiler_params=params(),
        name="first",
    )(base, inverse)


def hold(parts, stack=False):
    one = parts[0].shape
    shape = (len(parts), *one) if stack else (len(parts) * one[0], *one[1:])

    def kernel(*refs):
        *ins, out = refs
        for i, ref in enumerate(ins):
            if stack:
                out[i] = ref[...]
            else:
                out[i * one[0] : (i + 1) * one[0]] = ref[...]

    return pl.pallas_call(
        kernel,
        out_shape=jax.ShapeDtypeStruct(shape, parts[0].dtype),
        in_specs=[VMEM] * len(parts),
        out_specs=VMEM,
        compiler_params=params(),
        cost_estimate=pl.CostEstimate(
            flops=0, bytes_accessed=4 * len(parts) * one[0] * one[1], transcendentals=0
        ),
        name="hold",
    )(*parts)


def append(sc, known, last):
    n, c, b = known.shape

    def kernel(sc, known, last, out):
        @pl.when(sc[AT_Z] == n + 1)
        def _():
            out[:n] = known[...]
            out[n] = last[...]

    return pl.pallas_call(
        kernel,
        out_shape=jax.ShapeDtypeStruct((n + 1, c, b), BF),
        in_specs=[SMEM, VMEM, VMEM],
        out_specs=VMEM,
        compiler_params=params(),
        cost_estimate=pl.CostEstimate(
            flops=0, bytes_accessed=4 * (n + 1) * c * b, transcendentals=0
        ),
        name="append",
    )(sc, known, last)


def own_row(sc, solved):
    def kernel(sc, *refs):
        *ins, out = refs
        for z, ref in enumerate(ins):

            @pl.when((sc[AT_Z] == z) if z + 1 < len(ins) else (sc[AT_Z] >= z))
            def _():
                out[...] = ref[...]

    return pl.pallas_call(
        kernel,
        out_shape=jax.ShapeDtypeStruct(solved[0].shape, BF),
        in_specs=[SMEM] + [VMEM] * len(solved),
        out_specs=VMEM,
        compiler_params=params(),
        name="own_row",
    )(sc, *solved)


def collect(sc, rows, own, before, after_own):
    c, b = own.shape
    names, arrays = {}, []

    def ref_of(x):
        if id(x) not in names:
            names[id(x)] = len(arrays)
            arrays.append(x)
        return names[id(x)]

    def source(z, k):
        if k == z:
            return ref_of(own), None
        if k > z:
            return ref_of(after_own[k - z - 1]), None
        at = 0
        for x in before[z]:
            if len(x.shape) == 2:
                if at == k:
                    return ref_of(x), None
                at += 1
            else:
                if at <= k < at + x.shape[0]:
                    return ref_of(x), k - at
                at += x.shape[0]

    plan = [[source(z, k) for k in rows] for z in range(NZ)]

    def kernel(sc, *refs):
        *ins, out = refs
        for z in range(NZ):

            @pl.when(sc[AT_Z] == z)
            def _():
                for i, (which, at) in enumerate(plan[z]):
                    out[i] = ins[which][...] if at is None else ins[which][at]

    return pl.pallas_call(
        kernel,
        out_shape=jax.ShapeDtypeStruct((len(rows), c, b), BF),
        in_specs=[SMEM] + [VMEM] * len(arrays),
        out_specs=VMEM,
        compiler_params=params(),
        cost_estimate=pl.CostEstimate(
            flops=0, bytes_accessed=4 * len(rows) * c * b, transcendentals=0
        ),
        name="collect",
    )(sc, *arrays)


def spread_y(rows):
    half = rows.shape[0] // 2
    before = lax.ppermute(rows, "row", shift_y(1))
    behind = lax.ppermute(rows, "row", shift_y(-1))
    far_a = lax.ppermute(before[:half], "row", shift_y(1))
    far_b = lax.ppermute(behind[half:], "row", shift_y(-1))
    return rows, behind, far_a, far_b, before


def final_kernel(start, sc, every, behind, far_a, far_b, before, *refs):
    blocks0, blocks1, rest = refs[:4], refs[4:8], refs[8:]
    rhs, (out_s, out_r, low, eye) = rest[0], rest[-4:]
    i = pl.program_id(0)
    c = every.shape[1]
    half = far_a.shape[0]
    split = half < every.shape[0]

    @pl.when(i == 0)
    def _():
        out_r[...] = rhs[...]
        across = lax.broadcasted_iota(jnp.int32, eye.shape, 0)
        down = lax.broadcasted_iota(jnp.int32, eye.shape, 1)
        eye[...] = (across == down).astype(F32).astype(BF)

    def put(m, value):
        low[pl.ds(pl.multiple_of(sc[PLANE + m] * c, c), c), :] = value

    put(0, every[i])
    put(1, behind[i])
    put(3, before[i])

    @pl.when(i < half)
    def _():
        put(2, far_a[i])

    if split:

        @pl.when(i >= half)
        def _():
            put(2, far_b[i - half])

    solved = low[...]
    out_s[0] = lax.dot_general(eye[...], solved, NT, preferred_element_type=F32)

    def remove(q):
        def use(value):
            out_r[q, 0] -= value

        return use

    k = start + i
    times_block(sc, k, solved, blocks1, remove(1), flip=True)

    @pl.when(k < sc[ROWS])
    def _():
        times_block(sc, k, solved, blocks0, remove(0), flip=True)


def final(start, sc, steps, pieces, blocks0, blocks1, rhs, out_s=None):
    n, _, b = pieces[0].shape
    cols = rhs.shape[3]
    args = [sc, *pieces, *blocks0, *blocks1, rhs]
    specs = [SMEM] + [VMEM] * (len(args) - 1)
    alias = {}
    if out_s is not None:
        alias = {len(args): 0}
        args.append(out_s)
        specs.append(pl.BlockSpec(memory_space=pl.ANY))
    return pl.pallas_call(
        lambda *refs: final_kernel(start, *refs),
        out_shape=(
            jax.ShapeDtypeStruct((steps, b, cols), F32),
            jax.ShapeDtypeStruct(rhs.shape, F32),
        ),
        grid=(n,),
        in_specs=specs,
        out_specs=(
            pl.BlockSpec((1, b, cols), lambda i: (start + i, 0, 0)),
            pl.BlockSpec(rhs.shape, lambda i: (0, 0, 0, 0)),
        ),
        scratch_shapes=[pltpu.VMEM((cols, b), BF), pltpu.VMEM((b, b), BF)],
        input_output_aliases=alias,
        compiler_params=params(2 * LIMIT),
        cost_estimate=pl.CostEstimate(
            flops=6 * n * b * b * cols,
            bytes_accessed=4 * n * b * cols,
            transcendentals=0,
        ),
        name="final",
    )(*args)


def on_device(panel, rhs, inverse):
    steps = inverse.shape[0]
    block = panel.shape[2]
    quarter = rhs.shape[3] // NY
    half = block // 2
    row = lax.axis_index("row")
    col = lax.axis_index("col")
    y, z = row // NZ, row % NZ
    x, core = col // 2, col % 2

    j = jnp.arange(steps, dtype=jnp.int32)
    away = (j // 2 - x) % NX
    place = jnp.where(away == 3, 1, jnp.where(away == 1, 2, 0))
    kind = (away == 2) + 2 * (j % 2 != core)
    limit = jnp.where(y == NY - 1, z, 0)
    plane = (jnp.arange(NY, dtype=jnp.int32) + y) % NY
    sc = jnp.concatenate(
        [place, kind.astype(jnp.int32), limit[None], z[None], plane]
    ).astype(jnp.int32)

    panel0 = panel[0, 0, :, 0, :]
    top, low = panel0[:half], panel0[half:]
    up_a = lax.ppermute(top, "row", from_plane(3, 0))
    down_b = lax.ppermute(low, "row", from_plane(3, 2))
    up_b = lax.ppermute(low, "row", from_plane(3, 0) + [(row_of(1, 0), row_of(2, 0))])
    down_a = lax.ppermute(top, "row", from_plane(3, 2) + [(row_of(0, 0), row_of(1, 0))])
    far_a = lax.ppermute(up_a, "row", from_plane(0, 1))
    far_b = lax.ppermute(down_b, "row", from_plane(2, 1))

    def by_plane(at0, at1, at2, at3):
        return jnp.where(
            y == 3, at3, jnp.where(y == 0, at0, jnp.where(y == 2, at2, at1))
        )

    window = jnp.concatenate(
        [by_plane(up_a, far_a, down_a, top), by_plane(up_b, far_b, down_b, low)]
    )

    panel1 = panel[1, 0, :, 0, :]
    left1 = lax.ppermute(panel1, "col", shift_x(1))
    right1 = lax.ppermute(panel1, "col", shift_x(-1))
    window, left1, right1 = lax.optimization_barrier((window, left1, right1))

    left = lax.ppermute(window, "col", shift_x(1))
    right = lax.ppermute(window, "col", shift_x(-1))
    zt = rhs[0, 0].astype(BF).T
    zq = [zt[i * quarter : (i + 1) * quarter] for i in range(NY)]
    ready = [after(zq[0], up_a), after(zq[1], far_a), after(zq[2], down_b)]
    zr = [lax.ppermute(ready[i], "row", from_plane(3, i)) for i in range(NY - 1)]
    near1 = hold([after(panel1, zr[0]), left1, right1], stack=True)
    near_other1 = lax.ppermute(near1, "col", SWAP)
    left, right, near_other1, left1, right1, *zr = lax.optimization_barrier(
        (left, right, near_other1, left1[:half], right1[half:], *zr)
    )
    base = by_plane(*zr, zq[3])
    far_a, far_b = left[:half], right[half:]
    near = jnp.stack([after(window, far_a, far_b), left, right])
    far_a = lax.ppermute(far_a, "col", shift_x(1))
    far_b = lax.ppermute(far_b, "col", shift_x(-1))
    near_other = lax.ppermute(near, "col", SWAP)
    far_a, far_b, near_other = lax.optimization_barrier((far_a, far_b, near_other))
    far = hold([far_a, far_b])
    far_other = hold([lax.ppermute(far, "col", SWAP)])
    blocks0 = [near, far, near_other, far_other]

    fresh, inv = first(base, inverse)
    solved = [fresh]
    acc = base.astype(F32)
    known = None
    before = {0: []}
    back_a = []
    for t in range(1, steps):
        sent = None
        if t > 1:
            sent = lax.ppermute(known, "row", hop_z_early(t))
        last = lax.ppermute(fresh, "row", hop_z(t))
        if t > 1:
            acc, inv = early(t, sc, base, after(sent, fresh), inverse, blocks0)
            last = after(last, acc)
        if t == 2:
            left1, right1 = after(left1, acc), after(right1, acc)
            far1 = [
                lax.ppermute(left1, "col", shift_x(1)),
                lax.ppermute(right1, "col", shift_x(-1)),
            ]
        if t == 4:
            own_s = own_row(sc, solved)
        if 4 <= t <= 6:
            back_a.append(
                lax.ppermute((back_a or [own_s])[-1], "row", back_z(1, range(1, 4)))
            )
        if t > 4:
            last = after(last, back_a[t - 5])
        if t == 7:
            rows_a = collect(sc, range(4), own_s, {**before, 7: [sent]}, back_a)
            acc, rows_a = lax.optimization_barrier((acc, rows_a))
            before_a = lax.ppermute(rows_a, "row", shift_y(1))
            behind_a = lax.ppermute(rows_a, "row", shift_y(-1))
            far_a = lax.ppermute(rows_a, "row", shift_y(2))
            pieces_a = (rows_a, behind_a, far_a, far_a, before_a)
        fresh = step(t, sc, acc, last, inv, blocks0)
        solved.append(fresh)
        before[t] = [last] if t == 1 else [sent, last]
        known = last[None] if t == 1 else append(sc, sent, last)

    own_s = own_row(sc, solved)
    back = [lax.ppermute(own_s, "row", back_z(d, range(4, 8))) for d in range(1, 8)]
    rows_b = collect(sc, range(4, 8), own_s, before, back)
    far1 = hold([after(far1[0], rows_b), far1[1]])
    far_other1 = lax.ppermute(far1, "col", SWAP)
    blocks1 = [near1, far1, near_other1, far_other1]
    out_s, rest = final(0, sc, steps, pieces_a, blocks0, blocks1, rhs)
    rows_b = after(rows_b, before_a, behind_a)
    pieces_b = spread_y(rows_b)
    return tuple(final(4, sc, steps, pieces_b, blocks0, blocks1, rest, out_s))


def solution(mesh):
    placed = (P(None, "row", None, "col", None), P(None, "row", None, "col"), P())
    return jax.shard_map(
        on_device,
        mesh=mesh,
        in_specs=placed,
        out_specs=(P(None, None, "col"), P(None, "row", None, "col")),
        check_vma=False,
    )
```

```python
import jax
import jax.numpy as jnp
from jax import lax
from jax.experimental import pallas as pl
from jax.experimental.pallas import tpu as pltpu
from jax.sharding import PartitionSpec as P


NY, NZ, NX = 4, 8, 4
NT = (((1,), (1,)), ((), ()))
BF = jnp.bfloat16
F32 = jnp.float32


def row_of(y, z):
    return (y % NY) * NZ + z % NZ


def shift_y(d):
    return [(row_of(y, z), row_of(y + d, z)) for y in range(NY) for z in range(NZ)]


def from_plane(y, to):
    return [(row_of(y, z), row_of(to, z)) for z in range(NZ)]


def back_z(d, rows):
    return [(row_of(y, k), row_of(y, k - d)) for y in range(NY) for k in rows if k >= d]


def hop_z(t):
    return [(row_of(y, t - 1), row_of(y, t)) for y in range(NY)]


def hop_z_early(t):
    return hop_z(t) + [(row_of(0, t + 3), row_of(0, t + 4))]


def shift_x(d):
    n = 2 * NX
    return [(i, (i + 2 * d) % n) for i in range(n)]


SWAP = [(i, i ^ 1) for i in range(2 * NX)]


def after(x, *deps):
    return lax.optimization_barrier((x, *deps))[0]


VMEM = pl.BlockSpec(memory_space=pltpu.VMEM)
SMEM = pl.BlockSpec(memory_space=pltpu.SMEM)
ANY = pl.BlockSpec(memory_space=pl.ANY)
HBM = pl.BlockSpec(memory_space=pltpu.HBM)
LIMIT = 8 * 1024 * 1024
PLACE, KIND, ROWS, AT_Z, PLANE = 0, 8, 16, 17, 18


def params(limit=LIMIT):
    return pltpu.CompilerParams(vmem_limit_bytes=limit)


def times_block(sc, j, low, blocks, use, flip=False):
    place = sc[PLACE + j]
    for kind, ref in enumerate(blocks):

        @pl.when(sc[KIND + j] == kind)
        def _():
            block = ref[place] if len(ref.shape) == 3 else ref[...]
            pair = (block, low) if flip else (low, block)
            use(lax.dot_general(*pair, NT, preferred_element_type=F32))


def early_kernel(t, sc, base, solved, inverse, *refs):
    *blocks, out, inv, sem = refs

    @pl.when(sc[AT_Z] == t)
    def _():
        fetch = pltpu.make_async_copy(inverse.at[t], inv, sem)
        fetch.start()
        out[...] = base[...].astype(F32)

        def subtract(value):
            out[...] -= value

        @pl.loop(0, solved.shape[0])
        def _(j):
            times_block(sc, j, solved[j], blocks, subtract)

        fetch.wait()


def early(t, sc, base, solved, inverse, blocks):
    n = solved.shape[0]
    c, b = base.shape
    return pl.pallas_call(
        lambda *refs: early_kernel(t, *refs),
        out_shape=(
            jax.ShapeDtypeStruct((c, b), F32),
            jax.ShapeDtypeStruct((b, b), BF),
        ),
        in_specs=[SMEM, VMEM, VMEM, HBM] + [VMEM] * len(blocks),
        out_specs=(VMEM, VMEM),
        scratch_shapes=[pltpu.SemaphoreType.DMA],
        compiler_params=params(),
        cost_estimate=pl.CostEstimate(
            flops=2 * n * c * b * b, bytes_accessed=n * b * b, transcendentals=0
        ),
        name="early",
    )(sc, base, solved, inverse, *blocks)


def step_kernel(t, sc, acc, last, inv, *refs):
    *blocks, out, base = refs

    def subtract(value):
        base[...] = (acc[...] - value).astype(BF)

    @pl.when(sc[AT_Z] == t)
    def _():
        times_block(sc, t - 1, last[...], blocks, subtract)
        out[...] = lax.dot_general(
            base[...], inv[...], NT, preferred_element_type=F32
        ).astype(BF)


def step(t, sc, acc, last, inv, blocks):
    c, b = acc.shape
    return pl.pallas_call(
        lambda *refs: step_kernel(t, *refs),
        out_shape=jax.ShapeDtypeStruct((c, b), BF),
        in_specs=[SMEM] + [VMEM] * (3 + len(blocks)),
        out_specs=VMEM,
        scratch_shapes=[pltpu.VMEM((c, b), BF)],
        compiler_params=params(),
        cost_estimate=pl.CostEstimate(
            flops=4 * c * b * b, bytes_accessed=2 * b * b, transcendentals=0
        ),
        name="step",
    )(sc, acc, last, inv, *blocks)


def first_kernel(base, inverse, out, inv, here, sems):
    own = pltpu.make_async_copy(inverse.at[0], here, sems.at[0])
    following = pltpu.make_async_copy(inverse.at[1], inv, sems.at[1])
    own.start()
    following.start()
    own.wait()
    out[...] = lax.dot_general(
        base[...], here[...], NT, preferred_element_type=F32
    ).astype(BF)
    following.wait()


def first(base, inverse):
    square = inverse.shape[1:]
    return pl.pallas_call(
        first_kernel,
        out_shape=(
            jax.ShapeDtypeStruct(base.shape, BF),
            jax.ShapeDtypeStruct(square, BF),
        ),
        in_specs=[VMEM, HBM],
        out_specs=(VMEM, VMEM),
        scratch_shapes=[pltpu.VMEM(square, BF), pltpu.SemaphoreType.DMA((2,))],
        compiler_params=params(),
        name="first",
    )(base, inverse)


def hold(parts, stack=False):
    one = parts[0].shape
    shape = (len(parts), *one) if stack else (len(parts) * one[0], *one[1:])

    def kernel(*refs):
        *ins, out = refs
        for i, ref in enumerate(ins):
            if stack:
                out[i] = ref[...]
            else:
                out[i * one[0] : (i + 1) * one[0]] = ref[...]

    return pl.pallas_call(
        kernel,
        out_shape=jax.ShapeDtypeStruct(shape, parts[0].dtype),
        in_specs=[VMEM] * len(parts),
        out_specs=VMEM,
        compiler_params=params(),
        cost_estimate=pl.CostEstimate(
            flops=0, bytes_accessed=4 * len(parts) * one[0] * one[1], transcendentals=0
        ),
        name="hold",
    )(*parts)


def append(sc, known, last):
    n, c, b = known.shape

    def kernel(sc, known, last, out):
        @pl.when(sc[AT_Z] == n + 1)
        def _():
            out[:n] = known[...]
            out[n] = last[...]

    return pl.pallas_call(
        kernel,
        out_shape=jax.ShapeDtypeStruct((n + 1, c, b), BF),
        in_specs=[SMEM, VMEM, VMEM],
        out_specs=VMEM,
        compiler_params=params(),
        cost_estimate=pl.CostEstimate(
            flops=0, bytes_accessed=4 * (n + 1) * c * b, transcendentals=0
        ),
        name="append",
    )(sc, known, last)


def own_row(sc, solved):
    def kernel(sc, *refs):
        *ins, out = refs
        for z, ref in enumerate(ins):

            @pl.when((sc[AT_Z] == z) if z + 1 < len(ins) else (sc[AT_Z] >= z))
            def _():
                out[...] = ref[...]

    return pl.pallas_call(
        kernel,
        out_shape=jax.ShapeDtypeStruct(solved[0].shape, BF),
        in_specs=[SMEM] + [VMEM] * len(solved),
        out_specs=VMEM,
        compiler_params=params(),
        name="own_row",
    )(sc, *solved)


def collect(sc, rows, own, before, after_own):
    c, b = own.shape
    names, arrays = {}, []

    def ref_of(x):
        if id(x) not in names:
            names[id(x)] = len(arrays)
            arrays.append(x)
        return names[id(x)]

    def source(z, k):
        if k == z:
            return ref_of(own), None
        if k > z:
            return ref_of(after_own[k - z - 1]), None
        at = 0
        for x in before[z]:
            if len(x.shape) == 2:
                if at == k:
                    return ref_of(x), None
                at += 1
            else:
                if at <= k < at + x.shape[0]:
                    return ref_of(x), k - at
                at += x.shape[0]

    plan = [[source(z, k) for k in rows] for z in range(NZ)]

    def kernel(sc, *refs):
        *ins, out = refs
        for z in range(NZ):

            @pl.when(sc[AT_Z] == z)
            def _():
                for i, (which, at) in enumerate(plan[z]):
                    out[i] = ins[which][...] if at is None else ins[which][at]

    return pl.pallas_call(
        kernel,
        out_shape=jax.ShapeDtypeStruct((len(rows), c, b), BF),
        in_specs=[SMEM] + [VMEM] * len(arrays),
        out_specs=VMEM,
        compiler_params=params(),
        cost_estimate=pl.CostEstimate(
            flops=0, bytes_accessed=4 * len(rows) * c * b, transcendentals=0
        ),
        name="collect",
    )(sc, *arrays)


def spread_y(rows):
    half = rows.shape[0] // 2
    before = lax.ppermute(rows, "row", shift_y(1))
    behind = lax.ppermute(rows, "row", shift_y(-1))
    far_a = lax.ppermute(before[:half], "row", shift_y(1))
    far_b = lax.ppermute(behind[half:], "row", shift_y(-1))
    return rows, behind, far_a, far_b, before


def final_kernel(start, sc, every, behind, far_a, far_b, before, *refs):
    blocks0, blocks1, rest = refs[:4], refs[4:8], refs[8:]
    rhs, (out_s, out_r, low, eye) = rest[0], rest[-4:]
    i = pl.program_id(0)
    c = every.shape[1]
    half = far_a.shape[0]
    split = half < every.shape[0]

    @pl.when(i == 0)
    def _():
        out_r[...] = rhs[...]
        across = lax.broadcasted_iota(jnp.int32, eye.shape, 0)
        down = lax.broadcasted_iota(jnp.int32, eye.shape, 1)
        eye[...] = (across == down).astype(F32).astype(BF)

    def put(m, value):
        low[pl.ds(pl.multiple_of(sc[PLANE + m] * c, c), c), :] = value

    put(0, every[i])
    put(1, behind[i])
    put(3, before[i])

    @pl.when(i < half)
    def _():
        put(2, far_a[i])

    if split:

        @pl.when(i >= half)
        def _():
            put(2, far_b[i - half])

    solved = low[...]
    out_s[0] = lax.dot_general(eye[...], solved, NT, preferred_element_type=F32)

    def remove(q):
        def use(value):
            out_r[q, 0] -= value

        return use

    k = start + i
    times_block(sc, k, solved, blocks1, remove(1), flip=True)

    @pl.when(k < sc[ROWS])
    def _():
        times_block(sc, k, solved, blocks0, remove(0), flip=True)


def final(start, sc, steps, pieces, blocks0, blocks1, rhs, out_s=None):
    n, _, b = pieces[0].shape
    cols = rhs.shape[3]
    args = [sc, *pieces, *blocks0, *blocks1, rhs]
    specs = [SMEM] + [VMEM] * (len(args) - 1)
    alias = {}
    if out_s is not None:
        alias = {len(args): 0}
        args.append(out_s)
        specs.append(pl.BlockSpec(memory_space=pl.ANY))
    return pl.pallas_call(
        lambda *refs: final_kernel(start, *refs),
        out_shape=(
            jax.ShapeDtypeStruct((steps, b, cols), F32),
            jax.ShapeDtypeStruct(rhs.shape, F32),
        ),
        grid=(n,),
        in_specs=specs,
        out_specs=(
            pl.BlockSpec((1, b, cols), lambda i: (start + i, 0, 0)),
            pl.BlockSpec(rhs.shape, lambda i: (0, 0, 0, 0)),
        ),
        scratch_shapes=[pltpu.VMEM((cols, b), BF), pltpu.VMEM((b, b), BF)],
        input_output_aliases=alias,
        compiler_params=params(2 * LIMIT),
        cost_estimate=pl.CostEstimate(
            flops=6 * n * b * b * cols,
            bytes_accessed=4 * n * b * cols,
            transcendentals=0,
        ),
        name="final",
    )(*args)


def on_device(panel, rhs, inverse):
    steps = inverse.shape[0]
    block = panel.shape[2]
    quarter = rhs.shape[3] // NY
    half = block // 2
    row = lax.axis_index("row")
    col = lax.axis_index("col")
    y, z = row // NZ, row % NZ
    x, core = col // 2, col % 2

    j = jnp.arange(steps, dtype=jnp.int32)
    away = (j // 2 - x) % NX
    place = jnp.where(away == 3, 1, jnp.where(away == 1, 2, 0))
    kind = (away == 2) + 2 * (j % 2 != core)
    limit = jnp.where(y == NY - 1, z, 0)
    plane = (jnp.arange(NY, dtype=jnp.int32) + y) % NY
    sc = jnp.concatenate(
        [place, kind.astype(jnp.int32), limit[None], z[None], plane]
    ).astype(jnp.int32)

    panel0 = panel[0, 0, :, 0, :]
    top, low = panel0[:half], panel0[half:]
    up_a = lax.ppermute(top, "row", from_plane(3, 0))
    down_b = lax.ppermute(low, "row", from_plane(3, 2))
    up_b = lax.ppermute(low, "row", from_plane(3, 0) + [(row_of(1, 0), row_of(2, 0))])
    down_a = lax.ppermute(top, "row", from_plane(3, 2) + [(row_of(0, 0), row_of(1, 0))])
    far_a = lax.ppermute(up_a, "row", from_plane(0, 1))
    far_b = lax.ppermute(down_b, "row", from_plane(2, 1))

    def by_plane(at0, at1, at2, at3):
        return jnp.where(
            y == 3, at3, jnp.where(y == 0, at0, jnp.where(y == 2, at2, at1))
        )

    window = jnp.concatenate(
        [by_plane(up_a, far_a, down_a, top), by_plane(up_b, far_b, down_b, low)]
    )

    panel1 = panel[1, 0, :, 0, :]
    left1 = lax.ppermute(panel1, "col", shift_x(1))
    right1 = lax.ppermute(panel1, "col", shift_x(-1))
    window, left1, right1 = lax.optimization_barrier((window, left1, right1))

    left = lax.ppermute(window, "col", shift_x(1))
    right = lax.ppermute(window, "col", shift_x(-1))
    zt = rhs[0, 0].astype(BF).T
    zq = [zt[i * quarter : (i + 1) * quarter] for i in range(NY)]
    ready = [after(zq[0], up_a), after(zq[1], far_a), after(zq[2], down_b)]
    zr = [lax.ppermute(ready[i], "row", from_plane(3, i)) for i in range(NY - 1)]
    near1 = hold([after(panel1, zr[0]), left1, right1], stack=True)
    near_other1 = lax.ppermute(near1, "col", SWAP)
    left, right, near_other1, left1, right1, sc, *zr = lax.optimization_barrier(
        (left, right, near_other1, left1[:half], right1[half:], sc, *zr)
    )
    base = by_plane(*zr, zq[3])
    far_a, far_b = left[:half], right[half:]
    near = jnp.stack([after(window, far_a, far_b), left, right])
    far_a = lax.ppermute(far_a, "col", shift_x(1))
    far_b = lax.ppermute(far_b, "col", shift_x(-1))
    near_other = lax.ppermute(near, "col", SWAP)
    far_a, far_b, near_other = lax.optimization_barrier((far_a, far_b, near_other))
    far = jnp.concatenate([far_a, far_b])
    far_other = lax.ppermute(far, "col", SWAP)
    far_kept = hold([far_a, far_b])
    far_other = hold([after(far_other, far_kept)])
    blocks0 = [near, far_kept, near_other, far_other]

    fresh, inv = first(base, inverse)
    solved = [fresh]
    acc = base.astype(F32)
    known = None
    before = {0: []}
    back_a = []
    for t in range(1, steps):
        sent = None
        if t > 1:
            sent = lax.ppermute(known, "row", hop_z_early(t))
        last = lax.ppermute(fresh, "row", hop_z(t))
        if t > 1:
            acc, inv = early(t, sc, base, after(sent, fresh), inverse, blocks0)
            last = after(last, acc)
        if t == 2:
            left1, right1 = after(left1, acc), after(right1, acc)
            far1 = [
                lax.ppermute(left1, "col", shift_x(1)),
                lax.ppermute(right1, "col", shift_x(-1)),
            ]
        if t == 4:
            own_s = own_row(sc, solved)
        if 4 <= t <= 6:
            back_a.append(
                lax.ppermute((back_a or [own_s])[-1], "row", back_z(1, range(1, 4)))
            )
        if t > 4:
            last = after(last, back_a[t - 5])
        if t == 7:
            rows_a = collect(sc, range(4), own_s, {**before, 7: [sent]}, back_a)
            acc, rows_a = lax.optimization_barrier((acc, rows_a))
            before_a = lax.ppermute(rows_a, "row", shift_y(1))
            behind_a = lax.ppermute(rows_a, "row", shift_y(-1))
            far_a = lax.ppermute(rows_a, "row", shift_y(2))
            pieces_a = (rows_a, behind_a, far_a, far_a, before_a)
        fresh = step(t, sc, acc, last, inv, blocks0)
        solved.append(fresh)
        before[t] = [last] if t == 1 else [sent, last]
        known = last[None] if t == 1 else append(sc, sent, last)

    own_s = own_row(sc, solved)
    back = [lax.ppermute(own_s, "row", back_z(d, range(4, 8))) for d in range(1, 8)]
    rows_b = collect(sc, range(4, 8), own_s, before, back)
    far1 = hold([after(far1[0], rows_b), far1[1]])
    far_other1 = lax.ppermute(far1, "col", SWAP)
    blocks1 = [near1, far1, near_other1, far_other1]
    out_s, rest = final(0, sc, steps, pieces_a, blocks0, blocks1, rhs)
    rows_b = after(rows_b, before_a, behind_a)
    pieces_b = spread_y(rows_b)
    return tuple(final(4, sc, steps, pieces_b, blocks0, blocks1, rest, out_s))


def solution(mesh):
    placed = (P(None, "row", None, "col", None), P(None, "row", None, "col"), P())
    return jax.shard_map(
        on_device,
        mesh=mesh,
        in_specs=placed,
        out_specs=(P(None, None, "col"), P(None, "row", None, "col")),
        check_vma=False,
    )
```

```python
import jax
import jax.numpy as jnp
from jax import lax
from jax.experimental import pallas as pl
from jax.experimental.pallas import tpu as pltpu
from jax.sharding import PartitionSpec as P


NY, NZ, NX = 4, 8, 4
NT = (((1,), (1,)), ((), ()))
BF = jnp.bfloat16
F32 = jnp.float32


def row_of(y, z):
    return (y % NY) * NZ + z % NZ


def shift_y(d):
    return [(row_of(y, z), row_of(y + d, z)) for y in range(NY) for z in range(NZ)]


def from_plane(y, to):
    return [(row_of(y, z), row_of(to, z)) for z in range(NZ)]


def back_z(d, rows):
    return [(row_of(y, k), row_of(y, k - d)) for y in range(NY) for k in rows if k >= d]


def hop_z(t):
    return [(row_of(y, t - 1), row_of(y, t)) for y in range(NY)]


def hop_z_early(t):
    return hop_z(t) + [(row_of(0, t + 3), row_of(0, t + 4))]


def shift_x(d):
    n = 2 * NX
    return [(i, (i + 2 * d) % n) for i in range(n)]


SWAP = [(i, i ^ 1) for i in range(2 * NX)]


def after(x, *deps):
    return lax.optimization_barrier((x, *deps))[0]


VMEM = pl.BlockSpec(memory_space=pltpu.VMEM)
SMEM = pl.BlockSpec(memory_space=pltpu.SMEM)
ANY = pl.BlockSpec(memory_space=pl.ANY)
HBM = pl.BlockSpec(memory_space=pltpu.HBM)
LIMIT = 8 * 1024 * 1024
PLACE, KIND, ROWS, AT_Z, PLANE = 0, 8, 16, 17, 18


def params(limit=LIMIT):
    return pltpu.CompilerParams(vmem_limit_bytes=limit)


def times_block(sc, j, low, blocks, use, flip=False):
    place = sc[PLACE + j]
    for kind, ref in enumerate(blocks):

        @pl.when(sc[KIND + j] == kind)
        def _():
            block = ref[place] if len(ref.shape) == 3 else ref[...]
            pair = (block, low) if flip else (low, block)
            use(lax.dot_general(*pair, NT, preferred_element_type=F32))


def early_kernel(t, sc, base, solved, inverse, *refs):
    *blocks, out, inv, sem = refs

    @pl.when(sc[AT_Z] == t)
    def _():
        fetch = pltpu.make_async_copy(inverse.at[t], inv, sem)
        fetch.start()
        out[...] = base[...].astype(F32)

        def subtract(value):
            out[...] -= value

        @pl.loop(0, solved.shape[0])
        def _(j):
            times_block(sc, j, solved[j], blocks, subtract)

        fetch.wait()


def early(t, sc, base, solved, inverse, blocks):
    n = solved.shape[0]
    c, b = base.shape
    return pl.pallas_call(
        lambda *refs: early_kernel(t, *refs),
        out_shape=(
            jax.ShapeDtypeStruct((c, b), F32),
            jax.ShapeDtypeStruct((b, b), BF),
        ),
        in_specs=[SMEM, VMEM, VMEM, HBM] + [VMEM] * len(blocks),
        out_specs=(VMEM, VMEM),
        scratch_shapes=[pltpu.SemaphoreType.DMA],
        compiler_params=params(),
        cost_estimate=pl.CostEstimate(
            flops=2 * n * c * b * b, bytes_accessed=n * b * b, transcendentals=0
        ),
        name="early",
    )(sc, base, solved, inverse, *blocks)


def step_kernel(t, sc, acc, last, inv, *refs):
    *blocks, out, base = refs

    def subtract(value):
        base[...] = (acc[...] - value).astype(BF)

    @pl.when(sc[AT_Z] == t)
    def _():
        times_block(sc, t - 1, last[...], blocks, subtract)
        out[...] = lax.dot_general(
            base[...], inv[...], NT, preferred_element_type=F32
        ).astype(BF)


def step(t, sc, acc, last, inv, blocks):
    c, b = acc.shape
    return pl.pallas_call(
        lambda *refs: step_kernel(t, *refs),
        out_shape=jax.ShapeDtypeStruct((c, b), BF),
        in_specs=[SMEM] + [VMEM] * (3 + len(blocks)),
        out_specs=VMEM,
        scratch_shapes=[pltpu.VMEM((c, b), BF)],
        compiler_params=params(),
        cost_estimate=pl.CostEstimate(
            flops=4 * c * b * b, bytes_accessed=2 * b * b, transcendentals=0
        ),
        name="step",
    )(sc, acc, last, inv, *blocks)


def first_kernel(base, inverse, out, inv, here, sems):
    own = pltpu.make_async_copy(inverse.at[0], here, sems.at[0])
    following = pltpu.make_async_copy(inverse.at[1], inv, sems.at[1])
    own.start()
    following.start()
    own.wait()
    out[...] = lax.dot_general(
        base[...], here[...], NT, preferred_element_type=F32
    ).astype(BF)
    following.wait()


def first(base, inverse):
    square = inverse.shape[1:]
    return pl.pallas_call(
        first_kernel,
        out_shape=(
            jax.ShapeDtypeStruct(base.shape, BF),
            jax.ShapeDtypeStruct(square, BF),
        ),
        in_specs=[VMEM, HBM],
        out_specs=(VMEM, VMEM),
        scratch_shapes=[pltpu.VMEM(square, BF), pltpu.SemaphoreType.DMA((2,))],
        compiler_params=params(),
        name="first",
    )(base, inverse)


def hold(parts, stack=False):
    one = parts[0].shape
    shape = (len(parts), *one) if stack else (len(parts) * one[0], *one[1:])

    def kernel(*refs):
        *ins, out = refs
        for i, ref in enumerate(ins):
            if stack:
                out[i] = ref[...]
            else:
                out[i * one[0] : (i + 1) * one[0]] = ref[...]

    return pl.pallas_call(
        kernel,
        out_shape=jax.ShapeDtypeStruct(shape, parts[0].dtype),
        in_specs=[VMEM] * len(parts),
        out_specs=VMEM,
        compiler_params=params(),
        cost_estimate=pl.CostEstimate(
            flops=0, bytes_accessed=4 * len(parts) * one[0] * one[1], transcendentals=0
        ),
        name="hold",
    )(*parts)


def append(sc, known, last):
    n, c, b = known.shape

    def kernel(sc, known, last, out):
        @pl.when(sc[AT_Z] == n + 1)
        def _():
            out[:n] = known[...]
            out[n] = last[...]

    return pl.pallas_call(
        kernel,
        out_shape=jax.ShapeDtypeStruct((n + 1, c, b), BF),
        in_specs=[SMEM, VMEM, VMEM],
        out_specs=VMEM,
        compiler_params=params(),
        cost_estimate=pl.CostEstimate(
            flops=0, bytes_accessed=4 * (n + 1) * c * b, transcendentals=0
        ),
        name="append",
    )(sc, known, last)


def own_row(sc, solved):
    def kernel(sc, *refs):
        *ins, out = refs
        for z, ref in enumerate(ins):

            @pl.when((sc[AT_Z] == z) if z + 1 < len(ins) else (sc[AT_Z] >= z))
            def _():
                out[...] = ref[...]

    return pl.pallas_call(
        kernel,
        out_shape=jax.ShapeDtypeStruct(solved[0].shape, BF),
        in_specs=[SMEM] + [VMEM] * len(solved),
        out_specs=VMEM,
        compiler_params=params(),
        name="own_row",
    )(sc, *solved)


def collect(sc, rows, own, before, after_own):
    c, b = own.shape
    names, arrays = {}, []

    def ref_of(x):
        if id(x) not in names:
            names[id(x)] = len(arrays)
            arrays.append(x)
        return names[id(x)]

    def source(z, k):
        if k == z:
            return ref_of(own), None
        if k > z:
            return ref_of(after_own[k - z - 1]), None
        at = 0
        for x in before[z]:
            if len(x.shape) == 2:
                if at == k:
                    return ref_of(x), None
                at += 1
            else:
                if at <= k < at + x.shape[0]:
                    return ref_of(x), k - at
                at += x.shape[0]

    plan = [[source(z, k) for k in rows] for z in range(NZ)]

    def kernel(sc, *refs):
        *ins, out = refs
        for z in range(NZ):

            @pl.when(sc[AT_Z] == z)
            def _():
                for i, (which, at) in enumerate(plan[z]):
                    out[i] = ins[which][...] if at is None else ins[which][at]

    return pl.pallas_call(
        kernel,
        out_shape=jax.ShapeDtypeStruct((len(rows), c, b), BF),
        in_specs=[SMEM] + [VMEM] * len(arrays),
        out_specs=VMEM,
        compiler_params=params(),
        cost_estimate=pl.CostEstimate(
            flops=0, bytes_accessed=4 * len(rows) * c * b, transcendentals=0
        ),
        name="collect",
    )(sc, *arrays)


def spread_y(rows):
    half = rows.shape[0] // 2
    before = lax.ppermute(rows, "row", shift_y(1))
    behind = lax.ppermute(rows, "row", shift_y(-1))
    far_a = lax.ppermute(before[:half], "row", shift_y(1))
    far_b = lax.ppermute(behind[half:], "row", shift_y(-1))
    return rows, behind, far_a, far_b, before


def final_kernel(start, sc, every, behind, far_a, far_b, before, *refs):
    blocks0, blocks1, rest = refs[:4], refs[4:8], refs[8:]
    rhs, (out_s, out_r, low, eye) = rest[0], rest[-4:]
    i = pl.program_id(0)
    c = every.shape[1]
    half = far_a.shape[0]
    split = half < every.shape[0]

    @pl.when(i == 0)
    def _():
        out_r[...] = rhs[...]
        across = lax.broadcasted_iota(jnp.int32, eye.shape, 0)
        down = lax.broadcasted_iota(jnp.int32, eye.shape, 1)
        eye[...] = (across == down).astype(F32).astype(BF)

    def put(m, value):
        low[pl.ds(pl.multiple_of(sc[PLANE + m] * c, c), c), :] = value

    put(0, every[i])
    put(1, behind[i])
    put(3, before[i])

    @pl.when(i < half)
    def _():
        put(2, far_a[i])

    if split:

        @pl.when(i >= half)
        def _():
            put(2, far_b[i - half])

    solved = low[...]
    out_s[0] = lax.dot_general(eye[...], solved, NT, preferred_element_type=F32)

    def remove(q):
        def use(value):
            out_r[q, 0] -= value

        return use

    k = start + i
    times_block(sc, k, solved, blocks1, remove(1), flip=True)

    @pl.when(k < sc[ROWS])
    def _():
        times_block(sc, k, solved, blocks0, remove(0), flip=True)


def final(start, sc, steps, pieces, blocks0, blocks1, rhs, out_s=None):
    n, _, b = pieces[0].shape
    cols = rhs.shape[3]
    args = [sc, *pieces, *blocks0, *blocks1, rhs]
    specs = [SMEM] + [VMEM] * (len(args) - 1)
    alias = {}
    if out_s is not None:
        alias = {len(args): 0}
        args.append(out_s)
        specs.append(pl.BlockSpec(memory_space=pl.ANY))
    return pl.pallas_call(
        lambda *refs: final_kernel(start, *refs),
        out_shape=(
            jax.ShapeDtypeStruct((steps, b, cols), F32),
            jax.ShapeDtypeStruct(rhs.shape, F32),
        ),
        grid=(n,),
        in_specs=specs,
        out_specs=(
            pl.BlockSpec((1, b, cols), lambda i: (start + i, 0, 0)),
            pl.BlockSpec(rhs.shape, lambda i: (0, 0, 0, 0)),
        ),
        scratch_shapes=[pltpu.VMEM((cols, b), BF), pltpu.VMEM((b, b), BF)],
        input_output_aliases=alias,
        compiler_params=params(2 * LIMIT),
        cost_estimate=pl.CostEstimate(
            flops=6 * n * b * b * cols,
            bytes_accessed=4 * n * b * cols,
            transcendentals=0,
        ),
        name="final",
    )(*args)


def on_device(panel, rhs, inverse):
    steps = inverse.shape[0]
    block = panel.shape[2]
    quarter = rhs.shape[3] // NY
    half = block // 2
    row = lax.axis_index("row")
    col = lax.axis_index("col")
    y, z = row // NZ, row % NZ
    x, core = col // 2, col % 2

    j = jnp.arange(steps, dtype=jnp.int32)
    away = (j // 2 - x) % NX
    place = jnp.where(away == 3, 1, jnp.where(away == 1, 2, 0))
    kind = (away == 2) + 2 * (j % 2 != core)
    limit = jnp.where(y == NY - 1, z, 0)
    plane = (jnp.arange(NY, dtype=jnp.int32) + y) % NY
    sc = jnp.concatenate(
        [place, kind.astype(jnp.int32), limit[None], z[None], plane]
    ).astype(jnp.int32)

    panel0 = panel[0, 0, :, 0, :]
    top, low = panel0[:half], panel0[half:]
    up_a = lax.ppermute(top, "row", from_plane(3, 0))
    down_b = lax.ppermute(low, "row", from_plane(3, 2))
    up_b = lax.ppermute(low, "row", from_plane(3, 0) + [(row_of(1, 0), row_of(2, 0))])
    down_a = lax.ppermute(top, "row", from_plane(3, 2) + [(row_of(0, 0), row_of(1, 0))])
    far_a = lax.ppermute(up_a, "row", from_plane(0, 1))
    far_b = lax.ppermute(down_b, "row", from_plane(2, 1))

    def by_plane(at0, at1, at2, at3):
        return jnp.where(
            y == 3, at3, jnp.where(y == 0, at0, jnp.where(y == 2, at2, at1))
        )

    window = jnp.concatenate(
        [by_plane(up_a, far_a, down_a, top), by_plane(up_b, far_b, down_b, low)]
    )

    panel1 = panel[1, 0, :, 0, :]
    left1 = lax.ppermute(panel1, "col", shift_x(1))
    right1 = lax.ppermute(panel1, "col", shift_x(-1))
    window, left1, right1 = lax.optimization_barrier((window, left1, right1))

    left = lax.ppermute(window, "col", shift_x(1))
    right = lax.ppermute(window, "col", shift_x(-1))
    zt = rhs[0, 0].astype(BF).T
    zq = [zt[i * quarter : (i + 1) * quarter] for i in range(NY)]
    ready = [after(zq[0], up_a), after(zq[1], far_a), after(zq[2], down_b)]
    zr = [lax.ppermute(ready[i], "row", from_plane(3, i)) for i in range(NY - 1)]
    near1 = hold([after(panel1, *zr), left1, right1], stack=True)
    near_other1 = lax.ppermute(near1, "col", SWAP)
    left, right, near_other1, left1, right1, sc, *zr = lax.optimization_barrier(
        (left, right, near_other1, left1[:half], right1[half:], sc, *zr)
    )
    base = by_plane(*zr, zq[3])
    fresh, inv = first(base, inverse)
    last = lax.ppermute(fresh, "row", hop_z(1))
    far_a, far_b = left[:half], right[half:]
    near = jnp.stack([after(window, far_a, far_b), left, right])
    far_a = lax.ppermute(far_a, "col", shift_x(1))
    far_b = lax.ppermute(far_b, "col", shift_x(-1))
    near_other = lax.ppermute(near, "col", SWAP)
    far_a, far_b, near_other, last = lax.optimization_barrier(
        (far_a, far_b, near_other, last)
    )
    far = jnp.concatenate([far_a, far_b])
    far_other = lax.ppermute(far, "col", SWAP)
    far_kept = hold([far_a, far_b])
    far_other = hold([after(far_other, far_kept)])
    blocks0 = [near, far_kept, near_other, far_other]

    solved = [fresh]
    acc = base.astype(F32)
    known = None
    before = {0: []}
    back_a = []
    for t in range(1, steps):
        sent = None
        if t > 1:
            sent = lax.ppermute(known, "row", hop_z_early(t))
        if t > 1:
            last = lax.ppermute(fresh, "row", hop_z(t))
        if t > 1:
            acc, inv = early(t, sc, base, after(sent, fresh), inverse, blocks0)
            last = after(last, acc)
        if t == 2:
            left1, right1 = after(left1, acc), after(right1, acc)
            far1 = [
                lax.ppermute(left1, "col", shift_x(1)),
                lax.ppermute(right1, "col", shift_x(-1)),
            ]
        if t == 4:
            own_s = own_row(sc, solved)
        if 4 <= t <= 6:
            back_a.append(
                lax.ppermute((back_a or [own_s])[-1], "row", back_z(1, range(1, 4)))
            )
        if t > 4:
            last = after(last, back_a[t - 5])
        if t == 7:
            rows_a = collect(sc, range(4), own_s, {**before, 7: [sent]}, back_a)
            acc, rows_a = lax.optimization_barrier((acc, rows_a))
            before_a = lax.ppermute(rows_a, "row", shift_y(1))
            behind_a = lax.ppermute(rows_a, "row", shift_y(-1))
            far_a = lax.ppermute(rows_a, "row", shift_y(2))
            pieces_a = (rows_a, behind_a, far_a, far_a, before_a)
        fresh = step(t, sc, acc, last, inv, blocks0)
        solved.append(fresh)
        before[t] = [last] if t == 1 else [sent, last]
        known = last[None] if t == 1 else append(sc, sent, last)

    own_s = own_row(sc, solved)
    back = [lax.ppermute(own_s, "row", back_z(d, range(4, 8))) for d in range(1, 8)]
    rows_b = collect(sc, range(4, 8), own_s, before, back)
    far1 = hold([after(far1[0], rows_b), far1[1]])
    far_other1 = lax.ppermute(far1, "col", SWAP)
    blocks1 = [near1, far1, near_other1, far_other1]
    out_s, rest = final(0, sc, steps, pieces_a, blocks0, blocks1, rhs)
    rows_b = after(rows_b, before_a, behind_a)
    pieces_b = spread_y(rows_b)
    return tuple(final(4, sc, steps, pieces_b, blocks0, blocks1, rest, out_s))


def solution(mesh):
    placed = (P(None, "row", None, "col", None), P(None, "row", None, "col"), P())
    return jax.shard_map(
        on_device,
        mesh=mesh,
        in_specs=placed,
        out_specs=(P(None, None, "col"), P(None, "row", None, "col")),
        check_vma=False,
    )
```
